512 devices in a mesh: tiles: 64 (over y, x, core), pix: 8 (over z).
Axes of the slice: x: 4, y: 8, z: 8, core: 2. Of those that a mesh axis runs over, the one named last changes fastest.
Arguments:
- frames: bfloat16 [16384, 32768], P('tiles', 'pix'), may hold values from -60 to 60
- tile_valid: int32 [16384], P('tiles'), may hold values from 0 to 1
- foreground_blocks: int32 [16384], P('tiles'), may hold values from 0 to 8, as said below
- basis_start: float32 [16, 32768], P(None, 'pix'), may hold values from -12 to 12
- dark_start: float32 [32768], P('pix'), may hold values from -4 to 4
Outputs:
- flatfield_basis: float32 [16, 32768], P(None, 'pix')
- darkfield: float32 [32768], P('pix')
- coefficients: float32 [16384, 16], P('tiles')
The draws below stay inside these ranges and needn't reach their ends.
Inputs may be any that keep to these rules, and one draw needn't show every extreme that they name: `foreground_blocks`: some tile has exactly 8.
All inputs are finite; a program needn't handle non-finite values.
Results may differ from the reference program's by a relative error of at most 0.0003.
Values sent between devices are 32-bit elements; how exact they have to be, the bound alone decides.
A program may use at most 64 MiB of HBM per device.

```python
import math
import jax
import jax.numpy as jnp
from jax import lax

ROW_PX = 2048
RANK = 16
ITERS = 2
TILE_DEV = 256
NBLK = 16
PIXELS = 32768
TILES = 16384
N_TILES = 64


def masks_common(key):
    base = jax.random.fold_in(key, 101)
    usable = (jax.random.randint(jax.random.fold_in(base, 1), (TILES,), 0, 8) != 0).astype(jnp.int32)
    counts = jax.random.randint(jax.random.fold_in(base, 2), (TILES,), 0, NBLK // 2 + 1)
    chosen = jax.random.randint(jax.random.fold_in(base, 3), (), 0, TILES)
    counts = jnp.where(jnp.arange(TILES) == chosen, NBLK // 2, counts).astype(jnp.int32)
    return (usable, counts)


def factors_common(key):
    base = jax.random.fold_in(key, 202)
    latent = jax.random.normal(jax.random.fold_in(base, 1), (RANK, PIXELS), jnp.float32)
    image_scale = jnp.exp(jax.random.uniform(jax.random.fold_in(base, 2), (RANK, 1), jnp.float32, math.log(0.5), math.log(2.0)))
    pixel_basis = image_scale * (latent + 0.6 * latent[0:1])
    loads = jax.random.normal(jax.random.fold_in(base, 3), (TILES, RANK), jnp.float32)
    position = jnp.arange(TILES, dtype=jnp.float32) / TILES
    tile_scale = jnp.exp(math.log(3.0) * (position - 0.5))[:, None] * jnp.exp(jax.random.uniform(jax.random.fold_in(base, 4), (TILES, 1), jnp.float32, math.log(0.3), math.log(3.0)))
    tile_loads = tile_scale * (loads + 0.6 * loads[:, 0:1])
    return (tile_loads, pixel_basis, tile_scale)


def draw_frames(key, part):
    usable, counts = masks_common(key)
    tile_loads, pixel_basis, tile_scale = factors_common(key)
    base = jax.random.fold_in(key, 303)
    clean = jnp.zeros((TILES, PIXELS), jnp.float32)
    for index in range(RANK):
        clean = clean + tile_loads[:, index:index + 1] * pixel_basis[index:index + 1, :]
    noise = jax.random.truncated_normal(jax.random.fold_in(base, 1), -5.0, 5.0, (TILES, PIXELS), jnp.float32)
    place = jnp.arange(PIXELS, dtype=jnp.float32) / PIXELS
    pixel_scale = jnp.exp(math.log(3.0) * (place - 0.5)) * jnp.exp(jax.random.uniform(jax.random.fold_in(base, 2), (PIXELS,), jnp.float32, math.log(0.3), math.log(3.0)))
    true_dark = 0.5 * jax.random.truncated_normal(jax.random.fold_in(base, 3), -5.0, 5.0, (PIXELS,), jnp.float32)
    column = jnp.arange(PIXELS, dtype=jnp.int32) % ROW_PX // 128
    bright = (column[None, :] < counts[:, None]).astype(jnp.float32) * (3.0 + jax.random.truncated_normal(jax.random.fold_in(base, 4), -3.0, 3.0, (TILES, PIXELS), jnp.float32))
    garbage = 4.0 * jax.random.truncated_normal(jax.random.fold_in(base, 5), -5.0, 5.0, (TILES, PIXELS), jnp.float32)
    result = clean + true_dark[None, :] + 0.5 * tile_scale * pixel_scale[None, :] * noise + bright
    result = jnp.where(usable[:, None] == 1, result, garbage)
    return jnp.clip(result, -60.0, 60.0).astype(jnp.bfloat16)


def draw_tile_valid(key, part):
    return masks_common(key)[0]


def draw_foreground_blocks(key, part):
    return masks_common(key)[1]


def draw_basis_start(key, part):
    tile_loads, pixel_basis, tile_scale = factors_common(key)
    jitter = jax.random.normal(jax.random.fold_in(key, 404), (RANK, PIXELS), jnp.float32)
    return jnp.clip(pixel_basis + 0.3 * jitter, -12.0, 12.0)


def shard_levels(stream_key, shape, pieces, low, high):
    def one(axis_at, parts):
        draws = jax.random.uniform(jax.random.fold_in(jax.random.fold_in(stream_key, 6), axis_at), (parts,), jnp.float32, low / len(pieces), high / len(pieces))
        return jnp.repeat(jnp.exp(draws), shape[axis_at] // parts).reshape((-1,) + (1,) * (len(shape) - axis_at - 1))

    gain = one(*pieces[0])
    for cut in pieces[1:]:
        gain = gain * one(*cut)
    return gain


def scatter_about(key, extent, deviation, most, split=(), kind=jnp.bfloat16):
    values = jax.random.normal(key, extent, jnp.float32) * deviation
    if len(split) > 0:
        values = shard_levels(key, extent, split, -0.22, 0.18) * values
    return jnp.clip(values, min=-most, max=most).astype(kind)


def setup_inputs(seed: int = 0) -> dict:
    key_of = jax.random.split(jax.random.key(seed), 6)
    frames = draw_frames(jax.random.fold_in(key_of[5], 71), 0)
    tile_valid = draw_tile_valid(jax.random.fold_in(key_of[5], 71), 0)
    foreground_blocks = draw_foreground_blocks(jax.random.fold_in(key_of[5], 71), 0)
    basis_start = draw_basis_start(jax.random.fold_in(key_of[5], 71), 0)
    dark_start = scatter_about(key_of[4], (PIXELS,), 0.3, 4.0, ((0, 8),), jnp.float32)
    return dict(frames=frames, tile_valid=tile_valid, foreground_blocks=foreground_blocks, basis_start=basis_start, dark_start=dark_start)


precise = lax.Precision.HIGHEST
ridge_weight = 0.01

def solve_gram(gram_matrix, right_rows):
    factor = jnp.linalg.cholesky(gram_matrix)
    return jax.scipy.linalg.cho_solve((factor, True), right_rows)

def usable_mask(valid_rows, blocks_rows):
    column = jnp.arange(PIXELS, dtype=jnp.int32) % ROW_PX // 128
    return valid_rows[:, None].astype(jnp.float32) * (column[None, :] >= blocks_rows[:, None]).astype(jnp.float32)

def reference(frames, tile_valid, foreground_blocks, basis_start, dark_start):
    identity = jnp.eye(RANK, dtype=jnp.float32)
    frame_blocks = frames.reshape(N_TILES, TILE_DEV, PIXELS)
    valid_blocks = tile_valid.reshape(N_TILES, TILE_DEV)
    fore_blocks = foreground_blocks.reshape(N_TILES, TILE_DEV)
    basis = basis_start
    darkfield = dark_start
    coefficients = jnp.zeros((N_TILES, TILE_DEV, RANK), jnp.float32)
    for iteration in range(ITERS):
        gram_f = jnp.dot(basis, basis.T, precision=precise) / PIXELS + ridge_weight * identity

        def solve_block(packed):
            frame_rows, valid_rows, blocks_rows = packed
            shifted = frame_rows.astype(jnp.float32) - darkfield[None, :]
            projection = jnp.dot(shifted, basis.T, precision=precise) / PIXELS
            coef_rows = solve_gram(gram_f, projection.T).T
            residual = shifted - jnp.dot(coef_rows, basis, precision=precise)
            usable = usable_mask(valid_rows, blocks_rows)
            square_sum = jnp.sum(usable * residual * residual)
            valid_coef = coef_rows * valid_rows[:, None].astype(jnp.float32)
            coef_gram = jnp.dot(valid_coef.T, coef_rows, precision=precise)
            return (coef_rows, square_sum, coef_gram)
        coefficients, square_sums, coef_grams = lax.map(solve_block, (frame_blocks, valid_blocks, fore_blocks))
        spread = jnp.sum(square_sums) / (TILES * PIXELS) + 1e-05
        gram_c = jnp.sum(coef_grams, axis=0) / TILES + ridge_weight * identity

        def term_block(packed):
            frame_rows, valid_rows, blocks_rows, coef_rows = packed
            shifted = frame_rows.astype(jnp.float32) - darkfield[None, :]
            residual = shifted - jnp.dot(coef_rows, basis, precision=precise)
            usable = usable_mask(valid_rows, blocks_rows)
            weights = usable / (1.0 + residual * residual / (4.0 * spread))
            weighted = weights * residual
            return (jnp.dot(coef_rows.T, weighted, precision=precise), jnp.sum(weighted, axis=0), jnp.sum(weights, axis=0))
        basis_parts, dark_parts, weight_parts = lax.map(term_block, (frame_blocks, valid_blocks, fore_blocks, coefficients))
        basis_terms = jnp.sum(basis_parts, axis=0)
        dark_terms = jnp.sum(dark_parts, axis=0)
        weight_terms = jnp.sum(weight_parts, axis=0)
        basis = basis + solve_gram(gram_c, basis_terms / TILES)
        darkfield = darkfield + dark_terms / (weight_terms + 1.0)
    return (basis, darkfield, coefficients.reshape(TILES, RANK))
```

```python
import functools

import jax
import jax.numpy as jnp
from jax import lax
from jax.experimental import pallas as pl
from jax.experimental.pallas import tpu as pltpu
from jax.sharding import Mesh
from jax.sharding import PartitionSpec as P

ROW_PX = 2048
BLOCK = 128
ITERS = 2
TILES = ("tiles_0", "tiles_1", "tiles_2")
MESH = pl.DeviceIdType.MESH
HIGHEST = lax.Precision.HIGHEST
RIDGE = 0.01
F32 = jnp.float32
BF16 = jnp.bfloat16

NT = (((1,), (1,)), ((), ()))
NN = (((1,), (0,)), ((), ()))


def split2(x):
    high = x.astype(BF16)
    low = (x - high.astype(F32)).astype(BF16)
    return high, low


def inverse(a):
    rows = a.shape[0]
    lane = lax.broadcasted_iota(jnp.int32, a.shape, 1)
    sub = lax.broadcasted_iota(jnp.int32, a.shape, 0)
    for k in range(rows):
        scale = 1.0 / a[k : k + 1, k : k + 1]
        row = jnp.where(lane[:1] == k, 1.0, a[k : k + 1, :]) * scale
        col = a[:, k : k + 1]
        a = jnp.where(sub == k, row, jnp.where(lane == k, 0.0, a) - col * row)
    return a


def fit_kernel(
    sizes,
    frames_hbm,
    valid_ref,
    fore_ref,
    basis_ref,
    dark_ref,
    basis_out,
    dark_out,
    coef_out,
    frames,
    resid,
    stack,
    coef_lhs,
    term_lhs,
    limit,
    gram_z,
    proj_z,
    sq_z,
    sq_g,
    sq_y,
    cg_g,
    cg_y,
    part,
    from_core,
    x_src,
    x_in,
    y_src,
    y_in,
    full,
    load_sem,
    s_gram,
    r_gram,
    s_proj,
    r_proj,
    s_sqz,
    r_sqz,
    s_sqg,
    r_sqg,
    s_sqy,
    r_sqy,
    s_cgg,
    r_cgg,
    s_cgy,
    r_cgy,
    s_core,
    r_core,
    s_x,
    r_x,
    s_y,
    r_y,
    s_ya,
    r_ya,
    s_xa,
    r_xa,
    s_ca,
    r_ca,
):
    NY, NX, NC, NZ, T, PX, K = sizes
    NG = NX * NC
    GW = PX // NG
    NB = GW // BLOCK
    y, x, c, z = (lax.axis_index(n) for n in (*TILES, "pix"))
    gi = x * NC + c
    other = 1 - c
    tiles_all = T * NY * NX * NC
    pixels_all = PX * NZ

    def y_dev(yy):
        return {"tiles_0": yy}

    def x_dev(xx):
        return {"tiles_1": xx}

    def g_dev(g):
        return {"tiles_1": g // NC, "tiles_2": g % NC}

    def z_dev(zz):
        return {"pix": zz}

    def c_dev():
        return {"tiles_2": other}

    loads = [
        pltpu.make_async_copy(
            frames_hbm.at[:, pl.ds(g * GW, GW)], frames.at[:, pl.ds(g * GW, GW)], load_sem.at[g]
        )
        for g in range(NG)
    ]
    for load in loads:
        load.start()

    barrier = pltpu.get_barrier_semaphore()
    for size, me, dev in ((NZ, z, z_dev), (NG, gi, g_dev), (NY, y, y_dev)):
        for o in range(1, size):
            pl.semaphore_signal(
                barrier, inc=1, device_id=dev(lax.rem(me + o, size)), device_id_type=MESH
            )

    sent = []

    def copy(src, dst, ssem, rsem, dev):
        return pltpu.make_async_remote_copy(
            src_ref=src,
            dst_ref=dst,
            send_sem=ssem,
            recv_sem=rsem,
            device_id=dev,
            device_id_type=MESH,
        )

    def start(*args):
        made = copy(*args)
        made.start()
        sent.append(made)

    def to_all(buf, ssem, rsem, size, me, dev):
        for o in range(1, size):
            start(buf.at[me], buf.at[me], ssem.at[o], rsem.at[me], dev(lax.rem(me + o, size)))

    def from_all(buf, ssem, rsem, size, me, dev):
        for o in range(1, size):
            src = lax.rem(me + o, size)
            copy(buf.at[src], buf.at[src], ssem.at[o], rsem.at[src], dev(src)).wait_recv()

    def summed(buf, size):
        total = buf[0]
        for i in range(1, size):
            total = total + buf[i]
        return total

    valid_row = valid_ref[...].astype(F32)
    limit_row = jnp.where(valid_ref[...] > 0, fore_ref[...].astype(F32), 1000.0)
    limit[...] = jnp.broadcast_to(limit_row, (BLOCK, T)).T

    def usable(block):
        kind = lax.rem(z * (NG * NB) + block, ROW_PX // BLOCK).astype(F32)
        return limit[...] <= kind

    row16 = lax.broadcasted_iota(jnp.int32, (16, GW), 0)

    def cols_of(g):
        return pl.ds(pl.multiple_of(g * GW, GW), GW)

    def prepare(g, gram):
        cols = cols_of(g)
        high, low = split2(basis_out[:, cols])
        d = dark_out[:, cols]
        d_high = d.astype(BF16).astype(F32)
        d_mid = (d - d_high).astype(BF16).astype(F32)
        d_low = d - d_high - d_mid
        dark_rows = jnp.where(
            row16 == 0,
            d_high,
            jnp.where(row16 == 1, d_mid, jnp.where(row16 == 2, d_low, 0.0)),
        )
        pieces = jnp.concatenate([high, low, high, dark_rows.astype(BF16)], axis=0)
        stack[:, cols] = pieces
        return gram + lax.dot_general(pieces[: 2 * K], pieces, NT, preferred_element_type=F32)

    def project(g, proj):
        cols = cols_of(g)
        return proj + lax.dot_general(
            stack[: 2 * K, cols], frames[:, cols], NT, preferred_element_type=F32
        )

    gram0 = jnp.zeros((2 * K, 4 * K), F32)
    proj0 = jnp.zeros((2 * K, T), F32)

    basis_out[...] = basis_ref[...]
    dark_out[...] = dark_ref[...]
    for it in range(ITERS):
        for buf in (gram_z, cg_g):
            buf[it, pl.ds(z if buf is gram_z else gi, 1)] = jnp.zeros((1, K, BLOCK), F32)
    lane = lax.broadcasted_iota(jnp.int32, (K, BLOCK), 1)
    sub = lax.broadcasted_iota(jnp.int32, (K, BLOCK), 0)
    ridge = jnp.where(lane == sub, RIDGE, 0.0)

    gram = lax.fori_loop(0, NG, prepare, gram0)
    pl.semaphore_wait(barrier, (NZ - 1) + (NG - 1) + (NY - 1))

    for it in range(ITERS):
        last = it == ITERS - 1

        def at(ref):
            return ref.at[it]

        gram_z[it, pl.ds(z, 1), :, : 4 * K] = (gram[:K] + gram[K:])[None]
        to_all(at(gram_z), at(s_gram), at(r_gram), NZ, z, z_dev)
        if it == 0:
            proj = proj0
            for g in range(NG):
                loads[g].wait()
                proj = project(g, proj)
        proj_z[it, pl.ds(z, 1)] = (proj[:K] + proj[K:])[None]
        to_all(at(proj_z), at(s_proj), at(r_proj), NZ, z, z_dev)

        from_all(at(gram_z), at(s_gram), at(r_gram), NZ, z, z_dev)
        raw = summed(at(gram_z), NZ)
        dark_dot = jnp.sum(
            jnp.where((lane >= 3 * K) & (lane < 3 * K + 3), raw, 0.0), axis=1, keepdims=True
        )
        gram_f = jnp.where(lane < K, raw + pltpu.roll(raw, BLOCK - K, 1), 0.0) / pixels_all
        solver = inverse(gram_f + ridge)
        from_all(at(proj_z), at(s_proj), at(r_proj), NZ, z, z_dev)
        right = (summed(at(proj_z), NZ) - dark_dot) / pixels_all
        coef = lax.dot_general(
            solver[:, :K], right, NN, precision=HIGHEST, preferred_element_type=F32
        )
        if last:
            coef_out[...] = coef

        cg = lax.dot_general(
            coef * valid_row, coef, NT, precision=HIGHEST, preferred_element_type=F32
        )
        cg_g[it, pl.ds(gi, 1), :, :K] = cg[None]
        to_all(at(cg_g), at(s_cgg), at(r_cgg), NG, gi, g_dev)

        c_high = coef.astype(BF16).astype(F32)
        c_stack = jnp.concatenate(
            [c_high, c_high, coef - c_high, jnp.ones((K, T), F32)], axis=0
        )
        coef_lhs[...] = c_stack.T.astype(BF16)

        def residual(g, acc):
            cols = cols_of(g)
            fitted = lax.dot_general(
                coef_lhs[...], stack[:, cols], NN, preferred_element_type=F32
            )
            r = frames[:, cols].astype(F32) - fitted
            resid[:, cols] = r
            for j in range(NB):
                rj = r[:, j * BLOCK : (j + 1) * BLOCK]
                sq = jnp.where(usable(g * NB + j), rj * rj, 0.0)
                acc = acc + jnp.sum(sq.reshape(T // 8, 8, BLOCK), axis=0)
            return acc

        acc = lax.fori_loop(0, NG, residual, jnp.zeros((8, BLOCK), F32))
        sq_z[it, pl.ds(z, 1)] = jnp.sum(acc, axis=0, keepdims=True)[None]
        to_all(at(sq_z), at(s_sqz), at(r_sqz), NZ, z, z_dev)

        from_all(at(cg_g), at(s_cgg), at(r_cgg), NG, gi, g_dev)
        cg_y[it, pl.ds(y, 1)] = summed(at(cg_g), NG)[None]
        to_all(at(cg_y), at(s_cgy), at(r_cgy), NY, y, y_dev)

        from_all(at(sq_z), at(s_sqz), at(r_sqz), NZ, z, z_dev)
        sq_g[it, pl.ds(gi, 1)] = summed(at(sq_z), NZ)[None]
        to_all(at(sq_g), at(s_sqg), at(r_sqg), NG, gi, g_dev)
        from_all(at(sq_g), at(s_sqg), at(r_sqg), NG, gi, g_dev)
        sq_y[it, pl.ds(y, 1)] = summed(at(sq_g), NG)[None]
        to_all(at(sq_y), at(s_sqy), at(r_sqy), NY, y, y_dev)

        from_all(at(cg_y), at(s_cgy), at(r_cgy), NY, y, y_dev)
        gram_c = jnp.where(lane < K, summed(at(cg_y), NY) / tiles_all, 0.0)
        solver_c = inverse(gram_c + ridge)
        solved = lax.dot_general(
            solver_c[:, :K], coef, NN, precision=HIGHEST, preferred_element_type=F32
        ) / tiles_all
        high, low = split2(solved)
        term_lhs[...] = jnp.concatenate([high, low], axis=0)

        from_all(at(sq_y), at(s_sqy), at(r_sqy), NY, y, y_dev)
        square = jnp.sum(summed(at(sq_y), NY), axis=1, keepdims=True)
        spread = square / (float(tiles_all) * float(pixels_all)) + 1e-05
        rate = 1.0 / (4.0 * spread)

        def terms(cc, xx):
            g = cc * NX + xx
            for j in range(NB):
                cols = pl.ds(pl.multiple_of(g * GW + j * BLOCK, BLOCK), BLOCK)
                r = resid[:, cols]
                w = jnp.where(usable(g * NB + j), 1.0 / (1.0 + r * r * rate), 0.0)
                wr = w * r
                high, low = split2(wr)
                a = lax.dot_general(term_lhs[...], high, NN, preferred_element_type=F32)
                b = lax.dot_general(term_lhs[:K], low, NN, preferred_element_type=F32)
                tile = a[:K] + a[K:] + b
                part[it, cc, xx, pl.ds(2 * j, 2)] = tile.reshape(2, 8, BLOCK)
                part[it, cc, xx, NY, 2 * j : 2 * j + 1, :] = jnp.sum(wr, axis=0, keepdims=True)
                part[it, cc, xx, NY, 2 * j + 1 : 2 * j + 2, :] = jnp.sum(
                    w, axis=0, keepdims=True
                )

        def core_copy(xx):
            return copy(
                part.at[it, other, xx],
                from_core.at[it, xx],
                s_core.at[it, xx],
                r_core.at[it, xx],
                c_dev(),
            )

        def x_copy(xx):
            return copy(
                x_src.at[it, xx], x_in.at[it, x], s_x.at[it, xx], r_x.at[it, x], x_dev(xx)
            )

        @pl.loop(0, NX)
        def _(i):
            xx = lax.rem(x + 1 + i, NX)
            terms(other, xx)
            core_copy(xx).start()

        @pl.loop(0, NX)
        def _(i):
            xx = lax.rem(x + 1 + i, NX)
            terms(c, xx)
            core_copy(xx).wait_recv()
            both = part[it, c, xx] + from_core[it, xx]

            @pl.when(i < NX - 1)
            def _():
                x_src[it, xx] = both
                x_copy(xx).start()

            @pl.when(i == NX - 1)
            def _():
                x_in[it, x] = both

        for o in range(1, NX):
            src = lax.rem(x + o, NX)
            copy(
                x_src.at[it, src], x_in.at[it, src], s_x.at[it, src], r_x.at[it, src], x_dev(src)
            ).wait_recv()
        mine = summed(at(x_in), NX)
        for i in range(NY):
            y_src[it, i, 0] = mine[i]
            y_src[it, i, 1] = mine[NY]
        y_in[it, y] = y_src[it, y]
        for o in range(1, NY):
            yy = lax.rem(y + o, NY)
            start(y_src.at[it, yy], y_in.at[it, y], s_y.at[it, o], r_y.at[it, y], y_dev(yy))
        for o in range(1, NY):
            src = lax.rem(y + o, NY)
            copy(
                y_src.at[it, src], y_in.at[it, src], s_y.at[it, o], r_y.at[it, src], y_dev(src)
            ).wait_recv()
        done = summed(at(y_in), NY)
        full[it, c, x, y] = done[0]
        full[it, c, x, NY] = done[1]

        for o in range(1, NY):
            yy = lax.rem(y + o, NY)
            start(
                full.at[it, c, x, y],
                full.at[it, c, x, y],
                s_ya.at[it, o],
                r_ya.at[it, y],
                y_dev(yy),
            )
        for o in range(1, NY):
            src = lax.rem(y + o, NY)
            copy(
                full.at[it, c, x, src],
                full.at[it, c, x, src],
                s_ya.at[it, o],
                r_ya.at[it, src],
                y_dev(src),
            ).wait_recv()

        def gather_copy(xx, dev, ssem, rsem):
            return copy(full.at[it, c, xx], full.at[it, c, xx], ssem, rsem, dev)

        for o in range(1, NX):
            xx = lax.rem(x + o, NX)
            start(
                full.at[it, c, x],
                full.at[it, c, x],
                s_xa.at[it, o],
                r_xa.at[it, x],
                x_dev(xx),
            )
        start(full.at[it, c, x], full.at[it, c, x], s_ca.at[it, 0], r_ca.at[it, x], c_dev())
        for o in range(1, NX):
            src = lax.rem(x + o, NX)
            gather_copy(src, x_dev(src), s_xa.at[it, o], r_xa.at[it, src]).wait_recv()
            start(
                full.at[it, c, src],
                full.at[it, c, src],
                s_ca.at[it, o],
                r_ca.at[it, src],
                c_dev(),
            )

        def apply(cc, xx):
            g = cc * NX + xx
            for j in range(NB):
                cols = pl.ds(pl.multiple_of(g * GW + j * BLOCK, BLOCK), BLOCK)
                delta = full[it, cc, xx, pl.ds(2 * j, 2)].reshape(K, BLOCK)
                basis_out[:, cols] = basis_out[:, cols] + delta
                top = full[it, cc, xx, NY, 2 * j : 2 * j + 1, :]
                low = full[it, cc, xx, NY, 2 * j + 1 : 2 * j + 2, :]
                dark_out[:, cols] = dark_out[:, cols] + top / (low + 1.0)
            return g

        def own(i, carry):
            g = apply(c, i)
            if last:
                return carry
            gram, proj = carry
            return prepare(g, gram), project(g, proj)

        def partner(i, carry):
            copy(
                full.at[it, other, i],
                full.at[it, other, i],
                s_ca.at[it, 0],
                r_ca.at[it, i],
                c_dev(),
            ).wait_recv()
            g = apply(other, i)
            if last:
                return carry
            gram, proj = carry
            return prepare(g, gram), project(g, proj)

        carry = 0 if last else (gram0, proj0)
        carry = lax.fori_loop(0, NX, own, carry)
        carry = lax.fori_loop(0, NX, partner, carry)
        if not last:
            gram, proj = carry

        for xx in range(NX):
            core_copy(xx).wait_send()
        for o in range(1, NX):
            x_copy(lax.rem(x + o, NX)).wait_send()

    for made in sent:
        made.wait_send()


def local(frames, tile_valid, foreground_blocks, basis_start, dark_start):
    T, PX = frames.shape
    K = basis_start.shape[0]
    NY, NX, NC, NZ = (lax.axis_size(n) for n in (*TILES, "pix"))
    NG = NX * NC
    vmem = pl.BlockSpec(memory_space=pltpu.VMEM)
    dma = pltpu.SemaphoreType.DMA
    scratch = [
        pltpu.VMEM((T, PX), BF16),
        pltpu.VMEM((T, PX), F32),
        pltpu.VMEM((4 * K, PX), BF16),
        pltpu.VMEM((T, 4 * K), BF16),
        pltpu.VMEM((2 * K, T), BF16),
        pltpu.VMEM((T, BLOCK), F32),
        pltpu.VMEM((ITERS, NZ, K, BLOCK), F32),
        pltpu.VMEM((ITERS, NZ, K, T), F32),
        pltpu.VMEM((ITERS, NZ, 1, BLOCK), F32),
        pltpu.VMEM((ITERS, NG, 1, BLOCK), F32),
        pltpu.VMEM((ITERS, NY, 1, BLOCK), F32),
        pltpu.VMEM((ITERS, NG, K, BLOCK), F32),
        pltpu.VMEM((ITERS, NY, K, BLOCK), F32),
        pltpu.VMEM((ITERS, NC, NX, NY + 1, 8, BLOCK), F32),
        pltpu.VMEM((ITERS, NX, NY + 1, 8, BLOCK), F32),
        pltpu.VMEM((ITERS, NX, NY + 1, 8, BLOCK), F32),
        pltpu.VMEM((ITERS, NX, NY + 1, 8, BLOCK), F32),
        pltpu.VMEM((ITERS, NY, 2, 8, BLOCK), F32),
        pltpu.VMEM((ITERS, NY, 2, 8, BLOCK), F32),
        pltpu.VMEM((ITERS, NC, NX, NY + 1, 8, BLOCK), F32),
        dma((NG,)),
    ]
    for size in (NZ, NZ, NZ, NG, NY, NG, NY, NX, NX, NY, NY, NX, NX):
        scratch += [dma((ITERS, size)), dma((ITERS, size))]
    basis, dark, coef = pl.pallas_call(
        functools.partial(fit_kernel, (NY, NX, NC, NZ, T, PX, K)),
        out_shape=(
            jax.ShapeDtypeStruct((K, PX), F32),
            jax.ShapeDtypeStruct((1, PX), F32),
            jax.ShapeDtypeStruct((K, T), F32),
        ),
        in_specs=[pl.BlockSpec(memory_space=pl.ANY), vmem, vmem, vmem, vmem],
        out_specs=(vmem, vmem, vmem),
        scratch_shapes=scratch,
        compiler_params=pltpu.CompilerParams(
            collective_id=0, has_side_effects=True, vmem_limit_bytes=48 * 1024 * 1024
        ),
    )(
        frames,
        tile_valid.reshape(1, T),
        foreground_blocks.reshape(1, T),
        basis_start,
        dark_start.reshape(1, PX),
    )
    return basis, dark.reshape(PX), coef.T


def solution(mesh):
    finer = Mesh(
        mesh.devices.reshape(8, 4, 2, mesh.shape["pix"]), ("tiles_0", "tiles_1", "tiles_2", "pix")
    )
    in_specs = (P(TILES, "pix"), P(TILES), P(TILES), P(None, "pix"), P("pix"))
    out_specs = (P(None, "pix"), P("pix"), P(TILES, None))
    return jax.shard_map(local, mesh=finer, in_specs=in_specs, out_specs=out_specs, check_vma=False)
```

```python
import functools

import jax
import jax.numpy as jnp
from jax import lax
from jax.experimental import pallas as pl
from jax.experimental.pallas import tpu as pltpu
from jax.sharding import Mesh
from jax.sharding import PartitionSpec as P

ROW_PX = 2048
BLOCK = 128
ITERS = 2
TILES = ("tiles_0", "tiles_1", "tiles_2")
MESH = pl.DeviceIdType.MESH
HIGHEST = lax.Precision.HIGHEST
RIDGE = 0.01
F32 = jnp.float32
BF16 = jnp.bfloat16

NT = (((1,), (1,)), ((), ()))
NN = (((1,), (0,)), ((), ()))


def split2(x):
    high = x.astype(BF16)
    low = (x - high.astype(F32)).astype(BF16)
    return high, low


def inverse(a):
    rows = a.shape[0]
    lane = lax.broadcasted_iota(jnp.int32, a.shape, 1)
    sub = lax.broadcasted_iota(jnp.int32, a.shape, 0)
    for k in range(rows):
        scale = 1.0 / a[k : k + 1, k : k + 1]
        row = jnp.where(lane[:1] == k, 1.0, a[k : k + 1, :]) * scale
        col = a[:, k : k + 1]
        a = jnp.where(sub == k, row, jnp.where(lane == k, 0.0, a) - col * row)
    return a


def fit_kernel(
    sizes,
    frames_hbm,
    valid_hbm,
    fore_hbm,
    basis_hbm,
    dark_hbm,
    basis_out,
    dark_out,
    coef_out,
    frames,
    valid_ref,
    fore_ref,
    resid,
    stack,
    coef_lhs,
    term_lhs,
    limit,
    masked,
    fold,
    gram_z,
    proj_z,
    sq_z,
    sq_g,
    sq_y,
    cg_g,
    cg_y,
    part,
    from_core,
    x_src,
    x_in,
    y_src,
    y_in,
    sum_in,
    full,
    load_sem,
    small_sem,
    s_gram,
    r_gram,
    s_proj,
    r_proj,
    s_sqz,
    r_sqz,
    s_sqg,
    r_sqg,
    s_sqy,
    r_sqy,
    s_cgg,
    r_cgg,
    s_cgy,
    r_cgy,
    s_core,
    r_core,
    s_x,
    r_x,
    s_y,
    r_y,
    s_t,
    r_t,
    s_ya,
    r_ya,
    s_xa,
    r_xa,
    s_ca,
    r_ca,
):
    NY, NX, NC, NZ, T, PX, K = sizes
    NG = NX * NC
    GW = PX // NG
    NB = GW // BLOCK
    y, x, c, z = (lax.axis_index(n) for n in (*TILES, "pix"))
    gi = x * NC + c
    other = 1 - c
    tiles_all = T * NY * NX * NC
    pixels_all = PX * NZ

    def y_dev(yy):
        return {"tiles_0": yy}

    def x_dev(xx):
        return {"tiles_1": xx}

    def g_dev(g):
        return {"tiles_1": g // NC, "tiles_2": g % NC}

    def z_dev(zz):
        return {"pix": zz}

    def c_dev():
        return {"tiles_2": other}

    loads = [
        pltpu.make_async_copy(
            frames_hbm.at[:, pl.ds(g * GW, GW)], frames.at[:, pl.ds(g * GW, GW)], load_sem.at[g]
        )
        for g in range(NG)
    ]
    small = [
        pltpu.make_async_copy(src, dst, small_sem.at[i])
        for i, (src, dst) in enumerate(
            (
                (valid_hbm, valid_ref),
                (fore_hbm, fore_ref),
                (dark_hbm, dark_out),
                (basis_hbm, basis_out),
            )
        )
    ]
    for load in small + loads:
        load.start()

    barrier = pltpu.get_barrier_semaphore()
    for size, me, dev in ((NZ, z, z_dev), (NG, gi, g_dev), (NY, y, y_dev)):
        for o in range(1, size):
            pl.semaphore_signal(
                barrier, inc=1, device_id=dev(lax.rem(me + o, size)), device_id_type=MESH
            )

    sent = []

    def copy(src, dst, ssem, rsem, dev):
        return pltpu.make_async_remote_copy(
            src_ref=src,
            dst_ref=dst,
            send_sem=ssem,
            recv_sem=rsem,
            device_id=dev,
            device_id_type=MESH,
        )

    def start(*args):
        made = copy(*args)
        made.start()
        sent.append(made)

    def to_all(buf, ssem, rsem, size, me, dev):
        for o in range(1, size):
            start(buf.at[me], buf.at[me], ssem.at[o], rsem.at[me], dev(lax.rem(me + o, size)))

    def from_all(buf, ssem, rsem, size, me, dev):
        for o in range(1, size):
            src = lax.rem(me + o, size)
            copy(buf.at[src], buf.at[src], ssem.at[o], rsem.at[src], dev(src)).wait_recv()

    def summed(buf, size):
        total = buf[0]
        for i in range(1, size):
            total = total + buf[i]
        return total

    small[0].wait()
    small[1].wait()
    valid_row = valid_ref[...].astype(F32)
    limit_row = jnp.where(valid_ref[...] > 0, fore_ref[...].astype(F32), 1000.0)
    limit[...] = jnp.broadcast_to(limit_row, (BLOCK, T)).T

    kinds = ROW_PX // BLOCK
    for k in range(kinds):
        masked[k : k + 1, :] = jnp.sum(
            jnp.where(limit[...] > float(k), 1.0, 0.0), axis=0, keepdims=True
        )

    def kind_of(block):
        return lax.rem(z * (NG * NB) + block, kinds)

    row16 = lax.broadcasted_iota(jnp.int32, (16, GW), 0)

    def cols_of(g):
        return pl.ds(pl.multiple_of(g * GW, GW), GW)

    def prepare(g, gram):
        cols = cols_of(g)
        high, low = split2(basis_out[:, cols])
        d = dark_out[:, cols]
        d_high = d.astype(BF16).astype(F32)
        d_mid = (d - d_high).astype(BF16).astype(F32)
        d_low = d - d_high - d_mid
        dark_rows = jnp.where(
            row16 == 0,
            d_high,
            jnp.where(row16 == 1, d_mid, jnp.where(row16 == 2, d_low, 0.0)),
        )
        pieces = jnp.concatenate([high, low, high, dark_rows.astype(BF16)], axis=0)
        stack[:, cols] = pieces
        return gram + lax.dot_general(pieces[: 2 * K], pieces, NT, preferred_element_type=F32)

    def project(g, proj):
        cols = cols_of(g)
        return proj + lax.dot_general(
            stack[: 2 * K, cols], frames[:, cols], NT, preferred_element_type=F32
        )

    gram0 = jnp.zeros((2 * K, 4 * K), F32)
    proj0 = jnp.zeros((2 * K, T), F32)

    for it in range(ITERS):
        cg_g[it, pl.ds(gi, 1)] = jnp.zeros((1, K, BLOCK), F32)
    fold[...] = jnp.zeros((K, BLOCK), F32)
    lane = lax.broadcasted_iota(jnp.int32, (K, BLOCK), 1)
    sub = lax.broadcasted_iota(jnp.int32, (K, BLOCK), 0)
    ridge = jnp.where(lane == sub, RIDGE, 0.0)

    small[2].wait()
    small[3].wait()
    gram = lax.fori_loop(0, NG, prepare, gram0)
    pl.semaphore_wait(barrier, (NZ - 1) + (NG - 1) + (NY - 1))

    for it in range(ITERS):
        last = it == ITERS - 1

        def at(ref):
            return ref.at[it]

        fold[:, : 4 * K] = gram[:K] + gram[K:]
        gram_z[it, z] = fold[:8] + pltpu.roll(fold[8:], BLOCK // 2, 1)
        to_all(at(gram_z), at(s_gram), at(r_gram), NZ, z, z_dev)
        if it == 0:
            proj = proj0
            for g in range(NG):
                loads[g].wait()
                proj = project(g, proj)
        proj_z[it, pl.ds(z, 1)] = (proj[:K] + proj[K:])[None]
        to_all(at(proj_z), at(s_proj), at(r_proj), NZ, z, z_dev)

        from_all(at(gram_z), at(s_gram), at(r_gram), NZ, z, z_dev)
        folded = summed(at(gram_z), NZ)
        raw = jnp.concatenate([folded, pltpu.roll(folded, BLOCK // 2, 1)], axis=0)
        dark_dot = jnp.sum(
            jnp.where((lane >= 3 * K) & (lane < 3 * K + 3), raw, 0.0), axis=1, keepdims=True
        )
        gram_f = jnp.where(lane < K, raw + pltpu.roll(raw, BLOCK - K, 1), 0.0) / pixels_all
        solver = inverse(gram_f + ridge)
        from_all(at(proj_z), at(s_proj), at(r_proj), NZ, z, z_dev)
        right = (summed(at(proj_z), NZ) - dark_dot) / pixels_all
        coef = lax.dot_general(
            solver[:, :K], right, NN, precision=HIGHEST, preferred_element_type=F32
        )
        if last:
            coef_out[...] = coef

        cg = lax.dot_general(
            coef * valid_row, coef, NT, precision=HIGHEST, preferred_element_type=F32
        )
        cg_g[it, pl.ds(gi, 1), :, :K] = cg[None]
        to_all(at(cg_g), at(s_cgg), at(r_cgg), NG, gi, g_dev)

        c_high = coef.astype(BF16).astype(F32)
        c_stack = jnp.concatenate(
            [c_high, c_high, coef - c_high, jnp.ones((K, T), F32)], axis=0
        )
        coef_lhs[...] = c_stack.T.astype(BF16)

        def residual(g, acc):
            cols = cols_of(g)
            fitted = lax.dot_general(
                coef_lhs[...], stack[:, cols], NN, preferred_element_type=F32
            )
            r = frames[:, cols].astype(F32) - fitted
            for j in range(NB):
                kind = kind_of(g * NB + j).astype(F32)
                rj = jnp.where(limit[...] <= kind, r[:, j * BLOCK : (j + 1) * BLOCK], 0.0)
                resid[:, pl.ds(pl.multiple_of(g * GW + j * BLOCK, BLOCK), BLOCK)] = rj
                acc = acc + jnp.sum((rj * rj).reshape(T // 8, 8, BLOCK), axis=0)
            return acc

        acc = lax.fori_loop(0, NG, residual, jnp.zeros((8, BLOCK), F32))
        sq_z[it, pl.ds(z, 1)] = jnp.sum(acc, axis=0, keepdims=True)[None]
        to_all(at(sq_z), at(s_sqz), at(r_sqz), NZ, z, z_dev)

        from_all(at(cg_g), at(s_cgg), at(r_cgg), NG, gi, g_dev)
        cg_y[it, pl.ds(y, 1)] = summed(at(cg_g), NG)[None]
        to_all(at(cg_y), at(s_cgy), at(r_cgy), NY, y, y_dev)

        from_all(at(sq_z), at(s_sqz), at(r_sqz), NZ, z, z_dev)
        sq_g[it, pl.ds(gi, 1)] = summed(at(sq_z), NZ)[None]
        to_all(at(sq_g), at(s_sqg), at(r_sqg), NG, gi, g_dev)
        from_all(at(sq_g), at(s_sqg), at(r_sqg), NG, gi, g_dev)
        sq_y[it, pl.ds(y, 1)] = summed(at(sq_g), NG)[None]
        to_all(at(sq_y), at(s_sqy), at(r_sqy), NY, y, y_dev)

        from_all(at(cg_y), at(s_cgy), at(r_cgy), NY, y, y_dev)
        gram_c = jnp.where(lane < K, summed(at(cg_y), NY) / tiles_all, 0.0)
        solver_c = inverse(gram_c + ridge)
        solved = lax.dot_general(
            solver_c[:, :K], coef, NN, precision=HIGHEST, preferred_element_type=F32
        ) / tiles_all
        high, low = split2(solved)
        term_lhs[...] = jnp.concatenate([high, low], axis=0)

        from_all(at(sq_y), at(s_sqy), at(r_sqy), NY, y, y_dev)
        square = jnp.sum(summed(at(sq_y), NY), axis=1, keepdims=True)
        spread = square / (float(tiles_all) * float(pixels_all)) + 1e-05
        rate = 1.0 / (4.0 * spread)

        def terms(cc, xx):
            g = cc * NX + xx
            for j in range(NB):
                cols = pl.ds(pl.multiple_of(g * GW + j * BLOCK, BLOCK), BLOCK)
                r = resid[:, cols]
                w = 1.0 / (1.0 + r * r * rate)
                wr = w * r
                a = lax.dot_general(
                    term_lhs[...], wr.astype(BF16), NN, preferred_element_type=F32
                )
                part[it, cc, xx, pl.ds(2 * j, 2)] = (a[:K] + a[K:]).reshape(2, 8, BLOCK)
                part[it, cc, xx, NY, 2 * j : 2 * j + 1, :] = jnp.sum(wr, axis=0, keepdims=True)
                part[it, cc, xx, NY, 2 * j + 1 : 2 * j + 2, :] = (
                    jnp.sum(w, axis=0, keepdims=True) - masked[pl.ds(kind_of(g * NB + j), 1), :]
                )

        def core_copy(xx):
            return copy(
                part.at[it, other, xx],
                from_core.at[it, xx],
                s_core.at[it, xx],
                r_core.at[it, xx],
                c_dev(),
            )

        def x_copy(xx):
            return copy(
                x_src.at[it, xx], x_in.at[it, x], s_x.at[it, xx], r_x.at[it, x], x_dev(xx)
            )

        @pl.loop(0, NX)
        def _(i):
            xx = lax.rem(x + 1 + i, NX)
            terms(other, xx)
            core_copy(xx).start()

        @pl.loop(0, NX)
        def _(i):
            xx = lax.rem(x + 1 + i, NX)
            terms(c, xx)
            core_copy(xx).wait_recv()
            both = part[it, c, xx] + from_core[it, xx]

            @pl.when(i < NX - 1)
            def _():
                x_src[it, xx] = both
                x_copy(xx).start()

            @pl.when(i == NX - 1)
            def _():
                x_in[it, x] = both

        for o in range(1, NX):
            src = lax.rem(x + o, NX)
            copy(
                x_src.at[it, src], x_in.at[it, src], s_x.at[it, src], r_x.at[it, src], x_dev(src)
            ).wait_recv()
        mine = summed(at(x_in), NX)
        near_y = sorted(range(1, NY), key=lambda o: min(o, NY - o))
        near_x = sorted(range(1, NX), key=lambda o: min(o, NX - o))
        y_src[it] = mine[:NY]
        sum_in[it, y] = mine[NY]
        y_in[it, y] = y_src[it, y]
        for o in reversed(near_y):
            yy = lax.rem(y + o, NY)
            start(y_src.at[it, yy], y_in.at[it, y], s_y.at[it, o], r_y.at[it, y], y_dev(yy))
        to_all(at(sum_in), at(s_t), at(r_t), NY, y, y_dev)
        for o in near_y:
            src = lax.rem(y + o, NY)
            copy(
                y_src.at[it, src], y_in.at[it, src], s_y.at[it, o], r_y.at[it, src], y_dev(src)
            ).wait_recv()
        full[it, c, x, y] = summed(at(y_in), NY)

        def tile_copy(xx, tile, dev, ssem, rsem):
            where = full.at[it, c, xx, tile]
            return copy(where, where, ssem, rsem, dev)

        def begin(made):
            made.start()
            sent.append(made)

        def onward(tile):
            for o in reversed(near_x):
                begin(
                    tile_copy(
                        x,
                        tile,
                        x_dev(lax.rem(x + o, NX)),
                        s_xa.at[it, o, tile],
                        r_xa.at[it, x, tile],
                    )
                )
            to_core(x, tile)

        def to_core(xx, tile):
            begin(
                tile_copy(xx, tile, c_dev(), s_ca.at[it, xx, tile], r_ca.at[it, xx, tile])
            )

        for o in reversed(near_y):
            begin(
                tile_copy(x, y, y_dev(lax.rem(y + o, NY)), s_ya.at[it, o], r_ya.at[it, y])
            )
        onward(y)
        from_all(at(sum_in), at(s_t), at(r_t), NY, y, y_dev)
        full[it, c, x, NY] = summed(at(sum_in), NY)
        onward(NY)
        for o in near_y:
            src = lax.rem(y + o, NY)
            tile_copy(x, src, y_dev(src), s_ya.at[it, o], r_ya.at[it, src]).wait_recv()
            onward(src)

        def apply(cc, xx):
            g = cc * NX + xx
            for j in range(NB):
                cols = pl.ds(pl.multiple_of(g * GW + j * BLOCK, BLOCK), BLOCK)
                delta = full[it, cc, xx, pl.ds(2 * j, 2)].reshape(K, BLOCK)
                basis_out[:, cols] = basis_out[:, cols] + delta
                top = full[it, cc, xx, NY, 2 * j : 2 * j + 1, :]
                low = full[it, cc, xx, NY, 2 * j + 1 : 2 * j + 2, :]
                dark_out[:, cols] = dark_out[:, cols] + top / (low + 1.0)
            return g

        def take(cc, xx, carry):
            g = apply(cc, xx)
            if last:
                return carry
            gram, proj = carry
            return prepare(g, gram), project(g, proj)

        carry = 0 if last else (gram0, proj0)
        carry = take(c, x, carry)
        for tile in [y, NY] + [lax.rem(y + o, NY) for o in near_y]:
            for o in near_x:
                src = lax.rem(x + o, NX)
                tile_copy(
                    src, tile, x_dev(src), s_xa.at[it, o, tile], r_xa.at[it, src, tile]
                ).wait_recv()
                to_core(src, tile)

        def own(i, carry):
            return take(c, lax.rem(x + i, NX), carry)

        def partner(i, carry):
            xx = lax.rem(x + i, NX)
            for tile in range(NY + 1):
                where = full.at[it, other, xx, tile]
                copy(
                    where, where, s_ca.at[it, xx, tile], r_ca.at[it, xx, tile], c_dev()
                ).wait_recv()
            return take(other, xx, carry)

        carry = lax.fori_loop(1, NX, own, carry)
        carry = lax.fori_loop(0, NX, partner, carry)
        if not last:
            gram, proj = carry

        for xx in range(NX):
            core_copy(xx).wait_send()
        for o in range(1, NX):
            x_copy(lax.rem(x + o, NX)).wait_send()

    for made in sent:
        made.wait_send()


def local(frames, tile_valid, foreground_blocks, basis_start, dark_start):
    T, PX = frames.shape
    K = basis_start.shape[0]
    NY, NX, NC, NZ = (lax.axis_size(n) for n in (*TILES, "pix"))
    NG = NX * NC
    vmem = pl.BlockSpec(memory_space=pltpu.VMEM)
    dma = pltpu.SemaphoreType.DMA
    scratch = [
        pltpu.VMEM((T, PX), BF16),
        pltpu.VMEM((1, T), jnp.int32),
        pltpu.VMEM((1, T), jnp.int32),
        pltpu.VMEM((T, PX), F32),
        pltpu.VMEM((4 * K, PX), BF16),
        pltpu.VMEM((T, 4 * K), BF16),
        pltpu.VMEM((2 * K, T), BF16),
        pltpu.VMEM((T, BLOCK), F32),
        pltpu.VMEM((ROW_PX // BLOCK, BLOCK), F32),
        pltpu.VMEM((K, BLOCK), F32),
        pltpu.VMEM((ITERS, NZ, 8, BLOCK), F32),
        pltpu.VMEM((ITERS, NZ, K, T), F32),
        pltpu.VMEM((ITERS, NZ, 1, BLOCK), F32),
        pltpu.VMEM((ITERS, NG, 1, BLOCK), F32),
        pltpu.VMEM((ITERS, NY, 1, BLOCK), F32),
        pltpu.VMEM((ITERS, NG, K, BLOCK), F32),
        pltpu.VMEM((ITERS, NY, K, BLOCK), F32),
        pltpu.VMEM((ITERS, NC, NX, NY + 1, 8, BLOCK), F32),
        pltpu.VMEM((ITERS, NX, NY + 1, 8, BLOCK), F32),
        pltpu.VMEM((ITERS, NX, NY + 1, 8, BLOCK), F32),
        pltpu.VMEM((ITERS, NX, NY + 1, 8, BLOCK), F32),
        pltpu.VMEM((ITERS, NY, 8, BLOCK), F32),
        pltpu.VMEM((ITERS, NY, 8, BLOCK), F32),
        pltpu.VMEM((ITERS, NY, 8, BLOCK), F32),
        pltpu.VMEM((ITERS, NC, NX, NY + 1, 8, BLOCK), F32),
        dma((NG,)),
        dma((4,)),
    ]
    for size in (NZ, NZ, NZ, NG, NY, NG, NY, NX, NX, NY, NY, NY):
        scratch += [dma((ITERS, size)), dma((ITERS, size))]
    for _ in range(2):
        scratch += [dma((ITERS, NX, NY + 1)), dma((ITERS, NX, NY + 1))]
    basis, dark, coef = pl.pallas_call(
        functools.partial(fit_kernel, (NY, NX, NC, NZ, T, PX, K)),
        out_shape=(
            jax.ShapeDtypeStruct((K, PX), F32),
            jax.ShapeDtypeStruct((1, PX), F32),
            jax.ShapeDtypeStruct((K, T), F32),
        ),
        in_specs=[pl.BlockSpec(memory_space=pl.ANY)] * 5,
        out_specs=(vmem, vmem, vmem),
        scratch_shapes=scratch,
        compiler_params=pltpu.CompilerParams(
            collective_id=0, has_side_effects=True, vmem_limit_bytes=67043328
        ),
    )(
        frames,
        tile_valid.reshape(1, T),
        foreground_blocks.reshape(1, T),
        basis_start,
        dark_start.reshape(1, PX),
    )
    return basis, dark.reshape(PX), coef.T


def solution(mesh):
    finer = Mesh(
        mesh.devices.reshape(8, 4, 2, mesh.shape["pix"]), ("tiles_0", "tiles_1", "tiles_2", "pix")
    )
    in_specs = (P(TILES, "pix"), P(TILES), P(TILES), P(None, "pix"), P("pix"))
    out_specs = (P(None, "pix"), P("pix"), P(TILES, None))
    return jax.shard_map(local, mesh=finer, in_specs=in_specs, out_specs=out_specs, check_vma=False)
```

```python
import functools

import jax
import jax.numpy as jnp
from jax import lax
from jax.experimental import pallas as pl
from jax.experimental.pallas import tpu as pltpu
from jax.sharding import Mesh
from jax.sharding import PartitionSpec as P

ROW_PX = 2048
BLOCK = 128
ITERS = 2
FORE_MAX = 8
TILES = ("tiles_0", "tiles_1", "tiles_2")
MESH = pl.DeviceIdType.MESH
HIGHEST = lax.Precision.HIGHEST
RIDGE = 0.01
F32 = jnp.float32
BF16 = jnp.bfloat16

NT = (((1,), (1,)), ((), ()))
NN = (((1,), (0,)), ((), ()))


def split2(x):
    high = x.astype(BF16)
    low = (x - high.astype(F32)).astype(BF16)
    return high, low


def inverse(a):
    rows = a.shape[0]
    lane = lax.broadcasted_iota(jnp.int32, a.shape, 1)
    sub = lax.broadcasted_iota(jnp.int32, a.shape, 0)
    for k in range(rows):
        scale = 1.0 / a[k : k + 1, k : k + 1]
        row = jnp.where(lane[:1] == k, 1.0, a[k : k + 1, :]) * scale
        col = a[:, k : k + 1]
        a = jnp.where(sub == k, row, jnp.where(lane == k, 0.0, a) - col * row)
    return a


def cuts_of(NY):
    half = NY // 2 + 1
    return [(0, half), (half, NY + 1)]


def fit_kernel(
    sizes,
    frames_hbm,
    valid_hbm,
    fore_hbm,
    basis_hbm,
    dark_hbm,
    basis_out,
    dark_out,
    coef_out,
    frames,
    valid_ref,
    fore_ref,
    resid,
    stack,
    coef_lhs,
    term_lhs,
    limit,
    spot,
    floats,
    masked,
    fold,
    gram_z,
    proj_z,
    sq_z,
    sq_g,
    sq_y,
    cg_g,
    cg_y,
    part,
    from_core,
    x_src,
    x_in,
    y_src,
    y_in,
    sum_in,
    full,
    load_sem,
    small_sem,
    s_gram,
    r_gram,
    s_proj,
    r_proj,
    s_sqz,
    r_sqz,
    s_sqg,
    r_sqg,
    s_sqy,
    r_sqy,
    s_cgg,
    r_cgg,
    s_cgy,
    r_cgy,
    s_core,
    r_core,
    s_x,
    r_x,
    s_y,
    r_y,
    s_t,
    r_t,
    s_ya,
    r_ya,
    s_xa,
    r_xa,
    s_ca,
    r_ca,
):
    NY, NX, NC, NZ, T, PX, K = sizes
    NG = NX * NC
    GW = PX // NG
    NB = GW // BLOCK
    y, x, c, z = (lax.axis_index(n) for n in (*TILES, "pix"))
    gi = x * NC + c
    other = 1 - c
    tiles_all = T * NY * NX * NC
    pixels_all = PX * NZ

    def y_dev(yy):
        return {"tiles_0": yy}

    def x_dev(xx):
        return {"tiles_1": xx}

    def g_dev(g):
        return {"tiles_1": g // NC, "tiles_2": g % NC}

    def z_dev(zz):
        return {"pix": zz}

    def c_dev():
        return {"tiles_2": other}

    loads = [
        pltpu.make_async_copy(
            frames_hbm.at[:, pl.ds(g * GW, GW)], frames.at[:, pl.ds(g * GW, GW)], load_sem.at[g]
        )
        for g in range(NG)
    ]
    small = [
        pltpu.make_async_copy(src, dst, small_sem.at[i])
        for i, (src, dst) in enumerate(
            (
                (valid_hbm, valid_ref),
                (fore_hbm, fore_ref),
                (dark_hbm, dark_out),
                (basis_hbm, basis_out),
            )
        )
    ]
    for load in small + loads:
        load.start()

    barrier = pltpu.get_barrier_semaphore()
    for size, me, dev in ((NZ, z, z_dev), (NG, gi, g_dev), (NY, y, y_dev)):
        for o in range(1, size):
            pl.semaphore_signal(
                barrier, inc=1, device_id=dev(lax.rem(me + o, size)), device_id_type=MESH
            )

    near_y = sorted(range(1, NY), key=lambda o: min(o, NY - o))
    near_x = sorted(range(1, NX), key=lambda o: min(o, NX - o))
    slots = {0: 0, **{o: i + 1 for i, o in enumerate(near_y)}}
    cuts = cuts_of(NY)

    def slot_of(tile):
        o = lax.rem(tile - y + NY, NY)
        behind = o // (NY // 2 + 1)
        own = (NY - o) // NY
        return (1 - behind) * (2 * o - 1 + own) + behind * (2 * NY - 2 * o)

    sent = []

    def copy(src, dst, ssem, rsem, dev):
        return pltpu.make_async_remote_copy(
            src_ref=src,
            dst_ref=dst,
            send_sem=ssem,
            recv_sem=rsem,
            device_id=dev,
            device_id_type=MESH,
        )

    def start(*args):
        made = copy(*args)
        made.start()
        sent.append(made)

    def to_all(buf, ssem, rsem, size, me, dev):
        for o in range(1, size):
            start(buf.at[me], buf.at[me], ssem.at[o], rsem.at[me], dev(lax.rem(me + o, size)))

    def from_all(buf, ssem, rsem, size, me, dev):
        for o in range(1, size):
            src = lax.rem(me + o, size)
            copy(buf.at[src], buf.at[src], ssem.at[o], rsem.at[src], dev(src)).wait_recv()

    def summed(buf, size):
        total = buf[0]
        for i in range(1, size):
            total = total + buf[i]
        return total

    kinds = ROW_PX // BLOCK

    def kind_of(block):
        return lax.rem(z * (NG * NB) + block, kinds)

    def tables():
        small[0].wait()
        small[1].wait()
        valid_row = valid_ref[...].astype(F32)
        limit[...] = jnp.broadcast_to(fore_ref[...].astype(F32), (BLOCK, T)).T
        valid_tiles = jnp.broadcast_to(valid_row, (BLOCK, T)).T
        bad = 1.0 - valid_tiles
        for k in range(kinds):
            out = bad if k >= FORE_MAX else jnp.where(limit[...] > float(k), 1.0, bad)
            masked[k : k + 1, :] = jnp.sum(out, axis=0, keepdims=True)
        spot[...] = valid_tiles

        @pl.loop(0, NG * NB)
        def _(b):
            cols = pl.ds(pl.multiple_of(b * BLOCK, BLOCK), BLOCK)
            floats[:, cols] = frames[:, cols].astype(F32) * spot[...]

    row16 = lax.broadcasted_iota(jnp.int32, (16, GW), 0)

    def cols_of(g):
        return pl.ds(pl.multiple_of(g * GW, GW), GW)

    def prepare(g, gram):
        cols = cols_of(g)
        high, low = split2(basis_out[:, cols])
        d = dark_out[:, cols]
        d_high = d.astype(BF16).astype(F32)
        d_mid = (d - d_high).astype(BF16).astype(F32)
        d_low = d - d_high - d_mid
        dark_rows = jnp.where(
            row16 == 0,
            d_high,
            jnp.where(row16 == 1, d_mid, jnp.where(row16 == 2, d_low, 0.0)),
        )
        pieces = jnp.concatenate([high, low, high, dark_rows.astype(BF16)], axis=0)
        stack[:, cols] = pieces
        return gram + lax.dot_general(pieces[: 2 * K], pieces, NT, preferred_element_type=F32)

    def project(g, proj):
        cols = cols_of(g)
        return proj + lax.dot_general(
            stack[: 2 * K, cols], frames[:, cols], NT, preferred_element_type=F32
        )

    gram0 = jnp.zeros((2 * K, 4 * K), F32)
    proj0 = jnp.zeros((2 * K, T), F32)

    for it in range(ITERS):
        cg_g[it, pl.ds(gi, 1)] = jnp.zeros((1, K, BLOCK), F32)
    fold[...] = jnp.zeros((K, BLOCK), F32)
    lane = lax.broadcasted_iota(jnp.int32, (K, BLOCK), 1)
    sub = lax.broadcasted_iota(jnp.int32, (K, BLOCK), 0)
    ridge = jnp.where(lane == sub, RIDGE, 0.0)

    small[2].wait()
    small[3].wait()
    gram = lax.fori_loop(0, NG, prepare, gram0)
    pl.semaphore_wait(barrier, (NZ - 1) + (NG - 1) + (NY - 1))

    for it in range(ITERS):
        last = it == ITERS - 1

        def at(ref):
            return ref.at[it]

        fold[:, : 4 * K] = gram[:K] + gram[K:]
        gram_z[it, z] = fold[:8] + pltpu.roll(fold[8:], BLOCK // 2, 1)
        to_all(at(gram_z), at(s_gram), at(r_gram), NZ, z, z_dev)
        if it == 0:
            proj = proj0
            for g in range(NG):
                loads[g].wait()
                proj = project(g, proj)
        proj_z[it, pl.ds(z, 1)] = (proj[:K] + proj[K:])[None]
        to_all(at(proj_z), at(s_proj), at(r_proj), NZ, z, z_dev)

        if it == 0:
            tables()
        from_all(at(gram_z), at(s_gram), at(r_gram), NZ, z, z_dev)
        folded = summed(at(gram_z), NZ)
        raw = jnp.concatenate([folded, pltpu.roll(folded, BLOCK // 2, 1)], axis=0)
        dark_dot = jnp.sum(
            jnp.where((lane >= 3 * K) & (lane < 3 * K + 3), raw, 0.0), axis=1, keepdims=True
        )
        gram_f = jnp.where(lane < K, raw + pltpu.roll(raw, BLOCK - K, 1), 0.0) / pixels_all
        solver = inverse(gram_f + ridge)
        from_all(at(proj_z), at(s_proj), at(r_proj), NZ, z, z_dev)
        right = (summed(at(proj_z), NZ) - dark_dot) / pixels_all
        coef = lax.dot_general(
            solver[:, :K], right, NN, precision=HIGHEST, preferred_element_type=F32
        )
        if last:
            coef_out[...] = coef

        valid_row = valid_ref[...].astype(F32)
        c_high = coef.astype(BF16).astype(F32)
        c_stack = jnp.concatenate(
            [c_high, c_high, coef - c_high, jnp.ones((K, T), F32)], axis=0
        )
        coef_lhs[...] = (c_stack * valid_row).T.astype(BF16)

        aligned = (NX * NB) % kinds == 0

        def residual(cc, acc):
            for b in range(NX * NB):
                block = cc * (NX * NB) + b
                cols = pl.ds(pl.multiple_of(block * BLOCK, BLOCK), BLOCK)
                r = floats[:, cols] - lax.dot_general(
                    coef_lhs[...], stack[:, cols], NN, preferred_element_type=F32
                )
                kind = b % kinds if aligned else kind_of(block).astype(F32)
                if not aligned or kind < FORE_MAX:
                    r = jnp.where(limit[...] <= kind, r, 0.0)
                resid[:, cols] = r
                acc = acc + jnp.sum((r * r).reshape(T // 8, 8, BLOCK), axis=0)
            return acc

        acc = lax.fori_loop(0, NC, residual, jnp.zeros((8, BLOCK), F32))
        sq_z[it, pl.ds(z, 1)] = jnp.sum(acc, axis=0, keepdims=True)[None]
        to_all(at(sq_z), at(s_sqz), at(r_sqz), NZ, z, z_dev)

        cg = lax.dot_general(
            coef * valid_row, coef, NT, precision=HIGHEST, preferred_element_type=F32
        )
        cg_g[it, pl.ds(gi, 1), :, :K] = cg[None]
        to_all(at(cg_g), at(s_cgg), at(r_cgg), NG, gi, g_dev)
        from_all(at(cg_g), at(s_cgg), at(r_cgg), NG, gi, g_dev)
        cg_y[it, pl.ds(y, 1)] = summed(at(cg_g), NG)[None]
        to_all(at(cg_y), at(s_cgy), at(r_cgy), NY, y, y_dev)

        from_all(at(sq_z), at(s_sqz), at(r_sqz), NZ, z, z_dev)
        sq_g[it, pl.ds(gi, 1)] = summed(at(sq_z), NZ)[None]
        to_all(at(sq_g), at(s_sqg), at(r_sqg), NG, gi, g_dev)
        from_all(at(sq_g), at(s_sqg), at(r_sqg), NG, gi, g_dev)
        sq_y[it, pl.ds(y, 1)] = summed(at(sq_g), NG)[None]
        to_all(at(sq_y), at(s_sqy), at(r_sqy), NY, y, y_dev)

        from_all(at(cg_y), at(s_cgy), at(r_cgy), NY, y, y_dev)
        gram_c = jnp.where(lane < K, summed(at(cg_y), NY) / tiles_all, 0.0)
        solver_c = inverse(gram_c + ridge)
        solved = lax.dot_general(
            solver_c[:, :K], coef, NN, precision=HIGHEST, preferred_element_type=F32
        ) / tiles_all
        high, low = split2(solved)
        term_lhs[...] = jnp.concatenate([high, low], axis=0)

        from_all(at(sq_y), at(s_sqy), at(r_sqy), NY, y, y_dev)
        square = jnp.sum(summed(at(sq_y), NY), axis=1, keepdims=True)
        spread = square / (float(tiles_all) * float(pixels_all)) + 1e-05
        rate = 1.0 / (4.0 * spread)

        def terms(cc, xx):
            g = cc * NX + xx
            pair = min(2, NB)
            for first in range(0, NB, pair):
                sides = []
                for j in range(first, first + pair):
                    cols = pl.ds(pl.multiple_of(g * GW + j * BLOCK, BLOCK), BLOCK)
                    r = resid[:, cols]
                    w = 1.0 / (1.0 + r * r * rate)
                    wr = w * r
                    sides.append(wr.astype(BF16))
                    part[it, cc, xx, NY, 2 * j : 2 * j + 1, :] = jnp.sum(
                        wr, axis=0, keepdims=True
                    )
                    part[it, cc, xx, NY, 2 * j + 1 : 2 * j + 2, :] = (
                        jnp.sum(w, axis=0, keepdims=True)
                        - masked[pl.ds(kind_of(g * NB + j), 1), :]
                    )
                a = lax.dot_general(
                    term_lhs[...],
                    jnp.concatenate(sides, axis=1),
                    NN,
                    preferred_element_type=F32,
                )
                a = a[:K] + a[K:]
                for j in range(first, first + pair):
                    tile = a[:, (j - first) * BLOCK : (j - first + 1) * BLOCK]
                    part[it, cc, xx, pl.ds(2 * j, 2)] = tile.reshape(2, 8, BLOCK)

        def core_copy(xx):
            return copy(
                part.at[it, other, xx],
                from_core.at[it, xx],
                s_core.at[it, xx],
                r_core.at[it, xx],
                c_dev(),
            )

        def x_copy(xx):
            return copy(
                x_src.at[it, xx], x_in.at[it, x], s_x.at[it, xx], r_x.at[it, x], x_dev(xx)
            )

        order_x = list(reversed(near_x))
        for o in [*order_x, 0]:
            xx = lax.rem(x + o, NX)
            terms(other, xx)
            core_copy(xx).start()
        for o in [*order_x, 0]:
            xx = lax.rem(x + o, NX)
            terms(c, xx)
            core_copy(xx).wait_recv()
            both = part[it, c, xx] + from_core[it, xx]
            if o:
                x_src[it, xx] = both
                x_copy(xx).start()
            else:
                x_in[it, x] = both

        for o in range(1, NX):
            src = lax.rem(x + o, NX)
            copy(
                x_src.at[it, src], x_in.at[it, src], s_x.at[it, src], r_x.at[it, src], x_dev(src)
            ).wait_recv()
        mine = summed(at(x_in), NX)
        y_src[it] = mine[:NY]
        sum_in[it, y] = mine[NY]
        y_in[it, y] = y_src[it, y]
        for o in reversed(near_y):
            yy = lax.rem(y + o, NY)
            start(y_src.at[it, yy], y_in.at[it, y], s_y.at[it, o], r_y.at[it, y], y_dev(yy))
        to_all(at(sum_in), at(s_t), at(r_t), NY, y, y_dev)
        for o in near_y:
            src = lax.rem(y + o, NY)
            copy(
                y_src.at[it, src], y_in.at[it, src], s_y.at[it, o], r_y.at[it, src], y_dev(src)
            ).wait_recv()
        full[it, c, x, 0] = summed(at(y_in), NY)

        def chunk_copy(xx, cut, dev, ssem, rsem):
            low, high = cuts[cut]
            where = full.at[it, c, xx, pl.ds(low, high - low)]
            return copy(where, where, ssem, rsem, dev)

        def begin(made):
            made.start()
            sent.append(made)

        def to_core(xx, cut):
            begin(chunk_copy(xx, cut, c_dev(), s_ca.at[it, xx, cut], r_ca.at[it, xx, cut]))

        def onward(cut):
            for o in reversed(near_x):
                dev = x_dev(lax.rem(x + o, NX))
                begin(chunk_copy(x, cut, dev, s_xa.at[it, o, cut], r_xa.at[it, x, cut]))
            to_core(x, cut)

        def y_gather(o, yy, slot):
            return copy(
                full.at[it, c, x, 0],
                full.at[it, c, x, slot],
                s_ya.at[it, o],
                r_ya.at[it, slot],
                y_dev(yy),
            )

        for o in reversed(near_y):
            begin(y_gather(o, lax.rem(y + o, NY), slots[NY - o]))
        for cut, (low, high) in enumerate(cuts):
            if high == NY + 1:
                from_all(at(sum_in), at(s_t), at(r_t), NY, y, y_dev)
                full[it, c, x, NY] = summed(at(sum_in), NY)
            for o in near_y:
                if low <= slots[o] < high:
                    y_gather(o, lax.rem(y + o, NY), slots[o]).wait_recv()
            onward(cut)

        def apply(cc, xx):
            g = cc * NX + xx
            for j in range(NB):
                cols = pl.ds(pl.multiple_of(g * GW + j * BLOCK, BLOCK), BLOCK)
                for half in range(2):
                    rows = pl.ds(8 * half, 8)
                    delta = full[it, cc, xx, slot_of(2 * j + half)]
                    basis_out[rows, cols] = basis_out[rows, cols] + delta
                top = full[it, cc, xx, NY, 2 * j : 2 * j + 1, :]
                low = full[it, cc, xx, NY, 2 * j + 1 : 2 * j + 2, :]
                dark_out[:, cols] = dark_out[:, cols] + top / (low + 1.0)
            return g

        def take(cc, xx, carry):
            g = apply(cc, xx)
            if last:
                return carry
            gram, proj = carry
            return prepare(g, gram), project(g, proj)

        carry = 0 if last else (gram0, proj0)
        carry = take(c, x, carry)
        for cut in range(len(cuts)):
            for o in near_x:
                src = lax.rem(x + o, NX)
                chunk_copy(
                    src, cut, x_dev(src), s_xa.at[it, o, cut], r_xa.at[it, src, cut]
                ).wait_recv()
                to_core(src, cut)

        for o in near_x:
            carry = take(c, lax.rem(x + o, NX), carry)
        for o in [0, *near_x]:
            xx = lax.rem(x + o, NX)
            for cut, (low, high) in enumerate(cuts):
                where = full.at[it, other, xx, pl.ds(low, high - low)]
                copy(
                    where, where, s_ca.at[it, xx, cut], r_ca.at[it, xx, cut], c_dev()
                ).wait_recv()
            carry = take(other, xx, carry)
        if not last:
            gram, proj = carry

        for xx in range(NX):
            core_copy(xx).wait_send()
        for o in range(1, NX):
            x_copy(lax.rem(x + o, NX)).wait_send()

    for made in sent:
        made.wait_send()


def write_kernel(*refs):
    copies = [pltpu.make_async_copy(refs[i], refs[i + 3], refs[6].at[i]) for i in range(3)]
    for made in copies:
        made.start()
    for made in copies:
        made.wait()


def local(frames, tile_valid, foreground_blocks, basis_start, dark_start):
    T, PX = frames.shape
    K = basis_start.shape[0]
    NY, NX, NC, NZ = (lax.axis_size(n) for n in (*TILES, "pix"))
    NG = NX * NC
    vmem = pl.BlockSpec(memory_space=pltpu.VMEM)
    dma = pltpu.SemaphoreType.DMA
    scratch = [
        pltpu.VMEM((T, PX), BF16),
        pltpu.VMEM((1, T), jnp.int32),
        pltpu.VMEM((1, T), jnp.int32),
        pltpu.VMEM((T, PX), F32),
        pltpu.VMEM((4 * K, PX), BF16),
        pltpu.VMEM((T, 4 * K), BF16),
        pltpu.VMEM((2 * K, T), BF16),
        pltpu.VMEM((T, BLOCK), F32),
        pltpu.VMEM((T, BLOCK), F32),
        pltpu.VMEM((T, PX), F32),
        pltpu.VMEM((ROW_PX // BLOCK, BLOCK), F32),
        pltpu.VMEM((K, BLOCK), F32),
        pltpu.VMEM((ITERS, NZ, 8, BLOCK), F32),
        pltpu.VMEM((ITERS, NZ, K, T), F32),
        pltpu.VMEM((ITERS, NZ, 1, BLOCK), F32),
        pltpu.VMEM((ITERS, NG, 1, BLOCK), F32),
        pltpu.VMEM((ITERS, NY, 1, BLOCK), F32),
        pltpu.VMEM((ITERS, NG, K, BLOCK), F32),
        pltpu.VMEM((ITERS, NY, K, BLOCK), F32),
        pltpu.VMEM((ITERS, NC, NX, NY + 1, 8, BLOCK), F32),
        pltpu.VMEM((ITERS, NX, NY + 1, 8, BLOCK), F32),
        pltpu.VMEM((ITERS, NX, NY + 1, 8, BLOCK), F32),
        pltpu.VMEM((ITERS, NX, NY + 1, 8, BLOCK), F32),
        pltpu.VMEM((ITERS, NY, 8, BLOCK), F32),
        pltpu.VMEM((ITERS, NY, 8, BLOCK), F32),
        pltpu.VMEM((ITERS, NY, 8, BLOCK), F32),
        pltpu.VMEM((ITERS, NC, NX, NY + 1, 8, BLOCK), F32),
        dma((NG,)),
        dma((4,)),
    ]
    for size in (NZ, NZ, NZ, NG, NY, NG, NY, NX, NX, NY, NY, NY):
        scratch += [dma((ITERS, size)), dma((ITERS, size))]
    for _ in range(2):
        scratch += [dma((ITERS, NX, len(cuts_of(NY)))), dma((ITERS, NX, len(cuts_of(NY))))]
    basis, dark, coef = pl.pallas_call(
        functools.partial(fit_kernel, (NY, NX, NC, NZ, T, PX, K)),
        out_shape=(
            jax.ShapeDtypeStruct((K, PX), F32),
            jax.ShapeDtypeStruct((1, PX), F32),
            jax.ShapeDtypeStruct((K, T), F32),
        ),
        in_specs=[pl.BlockSpec(memory_space=pl.ANY)] * 5,
        out_specs=(vmem, vmem, vmem),
        scratch_shapes=scratch,
        compiler_params=pltpu.CompilerParams(
            collective_id=0, has_side_effects=True, vmem_limit_bytes=67043328 - 65536
        ),
    )(
        frames,
        tile_valid.reshape(1, T),
        foreground_blocks.reshape(1, T),
        basis_start,
        dark_start.reshape(1, PX),
    )
    results = (basis, dark, coef)
    basis, dark, coef = pl.pallas_call(
        write_kernel,
        out_shape=tuple(jax.ShapeDtypeStruct(r.shape, r.dtype) for r in results),
        in_specs=[vmem] * 3,
        out_specs=[pl.BlockSpec(memory_space=pltpu.HBM)] * 3,
        scratch_shapes=[dma((3,))],
    )(*results)
    return basis, dark.reshape(PX), coef.T


def solution(mesh):
    finer = Mesh(
        mesh.devices.reshape(8, 4, 2, mesh.shape["pix"]), ("tiles_0", "tiles_1", "tiles_2", "pix")
    )
    in_specs = (P(TILES, "pix"), P(TILES), P(TILES), P(None, "pix"), P("pix"))
    out_specs = (P(None, "pix"), P("pix"), P(TILES, None))
    return jax.shard_map(local, mesh=finer, in_specs=in_specs, out_specs=out_specs, check_vma=False)
```

```python
import functools

import jax
import jax.numpy as jnp
from jax import lax
from jax.experimental import pallas as pl
from jax.experimental.pallas import tpu as pltpu
from jax.sharding import Mesh
from jax.sharding import PartitionSpec as P

ROW_PX = 2048
BLOCK = 128
ITERS = 2
FORE_MAX = 8
TILES = ("tiles_0", "tiles_1", "tiles_2")
MESH = pl.DeviceIdType.MESH
HIGHEST = lax.Precision.HIGHEST
RIDGE = 0.01
F32 = jnp.float32
BF16 = jnp.bfloat16

NT = (((1,), (1,)), ((), ()))
NN = (((1,), (0,)), ((), ()))


def split2(x):
    high = x.astype(BF16)
    low = (x - high.astype(F32)).astype(BF16)
    return high, low


def inverse(a):
    rows = a.shape[0]
    lane = lax.broadcasted_iota(jnp.int32, a.shape, 1)
    sub = lax.broadcasted_iota(jnp.int32, a.shape, 0)
    for k in range(rows):
        scale = 1.0 / a[k : k + 1, k : k + 1]
        row = jnp.where(lane[:1] == k, 1.0, a[k : k + 1, :]) * scale
        col = a[:, k : k + 1]
        a = jnp.where(sub == k, row, jnp.where(lane == k, 0.0, a) - col * row)
    return a


def cuts_of(NY):
    half = NY // 2 + 1
    return [(0, half), (half, NY + 1)]


def fit_kernel(
    sizes,
    frames_hbm,
    valid_hbm,
    fore_hbm,
    basis_hbm,
    dark_hbm,
    basis_out,
    dark_out,
    coef_out,
    frames,
    valid_ref,
    fore_ref,
    resid,
    stack,
    coef_lhs,
    term_lhs,
    limit,
    spot,
    floats,
    masked,
    fold,
    gram_z,
    proj_z,
    sq_z,
    sq_g,
    sq_y,
    cg_g,
    cg_y,
    part,
    from_core,
    x_src,
    x_in,
    y_src,
    y_in,
    sum_in,
    full,
    load_sem,
    small_sem,
    s_gram,
    r_gram,
    s_proj,
    r_proj,
    s_sqz,
    r_sqz,
    s_sqg,
    r_sqg,
    s_sqy,
    r_sqy,
    s_cgg,
    r_cgg,
    s_cgy,
    r_cgy,
    s_core,
    r_core,
    s_x,
    r_x,
    s_y,
    r_y,
    s_t,
    r_t,
    s_ya,
    r_ya,
    s_xa,
    r_xa,
    s_ca,
    r_ca,
):
    NY, NX, NC, NZ, T, PX, K = sizes
    NG = NX * NC
    GW = PX // NG
    NB = GW // BLOCK
    y, x, c, z = (lax.axis_index(n) for n in (*TILES, "pix"))
    gi = x * NC + c
    other = 1 - c
    tiles_all = T * NY * NX * NC
    pixels_all = PX * NZ

    def y_dev(yy):
        return {"tiles_0": yy}

    def x_dev(xx):
        return {"tiles_1": xx}

    def g_dev(g):
        return {"tiles_1": g // NC, "tiles_2": g % NC}

    def z_dev(zz):
        return {"pix": zz}

    def c_dev():
        return {"tiles_2": other}

    loads = [
        pltpu.make_async_copy(
            frames_hbm.at[:, pl.ds(g * GW, GW)], frames.at[:, pl.ds(g * GW, GW)], load_sem.at[g]
        )
        for g in range(NG)
    ]
    small = [
        pltpu.make_async_copy(src, dst, small_sem.at[i])
        for i, (src, dst) in enumerate(
            (
                (valid_hbm, valid_ref),
                (fore_hbm, fore_ref),
                (dark_hbm, dark_out),
                (basis_hbm, basis_out),
            )
        )
    ]
    for load in small + loads:
        load.start()

    barrier = pltpu.get_barrier_semaphore()
    for size, me, dev in ((NZ, z, z_dev), (NG, gi, g_dev), (NY, y, y_dev)):
        for o in range(1, size):
            pl.semaphore_signal(
                barrier, inc=1, device_id=dev(lax.rem(me + o, size)), device_id_type=MESH
            )

    near_y = sorted(range(1, NY), key=lambda o: min(o, NY - o))
    near_x = sorted(range(1, NX), key=lambda o: min(o, NX - o))
    slots = {0: 0, **{o: i + 1 for i, o in enumerate(near_y)}}
    cuts = cuts_of(NY)

    def slot_of(tile):
        o = lax.rem(tile - y + NY, NY)
        behind = o // (NY // 2 + 1)
        own = (NY - o) // NY
        return (1 - behind) * (2 * o - 1 + own) + behind * (2 * NY - 2 * o)

    sent = []

    def copy(src, dst, ssem, rsem, dev):
        return pltpu.make_async_remote_copy(
            src_ref=src,
            dst_ref=dst,
            send_sem=ssem,
            recv_sem=rsem,
            device_id=dev,
            device_id_type=MESH,
        )

    def whole(buf, ssem, rsem, size, me, dev):
        every = buf.at[pl.ds(0, size - 1)]
        return copy(every, every, ssem, rsem, dev(lax.rem(me + 1, size)))

    def to_all(buf, ssem, rsem, size, me, dev):
        for o in range(1, size):
            copy(buf.at[me], buf.at[me], ssem, rsem, dev(lax.rem(me + o, size))).start()
        sent.append(whole(buf, ssem, rsem, size, me, dev))

    def from_all(buf, ssem, rsem, size, me, dev):
        whole(buf, ssem, rsem, size, me, dev).wait_recv()

    def summed(buf, size):
        total = buf[0]
        for i in range(1, size):
            total = total + buf[i]
        return total

    kinds = ROW_PX // BLOCK

    def kind_of(block):
        return lax.rem(z * (NG * NB) + block, kinds)

    def tables():
        small[0].wait()
        small[1].wait()
        valid_row = valid_ref[...].astype(F32)
        limit[...] = jnp.broadcast_to(fore_ref[...].astype(F32), (BLOCK, T)).T
        valid_tiles = jnp.broadcast_to(valid_row, (BLOCK, T)).T
        bad = 1.0 - valid_tiles
        for k in range(kinds):
            out = bad if k >= FORE_MAX else jnp.where(limit[...] > float(k), 1.0, bad)
            masked[k : k + 1, :] = jnp.sum(out, axis=0, keepdims=True)
        spot[...] = valid_tiles

        @pl.loop(0, NG * NB)
        def _(b):
            cols = pl.ds(pl.multiple_of(b * BLOCK, BLOCK), BLOCK)
            floats[:, cols] = frames[:, cols].astype(F32) * spot[...]

    row16 = lax.broadcasted_iota(jnp.int32, (16, GW), 0)

    def cols_of(g):
        return pl.ds(pl.multiple_of(g * GW, GW), GW)

    def prepare(g, gram):
        cols = cols_of(g)
        high, low = split2(basis_out[:, cols])
        d = dark_out[:, cols]
        d_high = d.astype(BF16).astype(F32)
        d_mid = (d - d_high).astype(BF16).astype(F32)
        d_low = d - d_high - d_mid
        dark_rows = jnp.where(
            row16 == 0,
            d_high,
            jnp.where(row16 == 1, d_mid, jnp.where(row16 == 2, d_low, 0.0)),
        )
        pieces = jnp.concatenate([high, low, high, dark_rows.astype(BF16)], axis=0)
        stack[:, cols] = pieces
        return gram + lax.dot_general(pieces[: 2 * K], pieces, NT, preferred_element_type=F32)

    def project(g, proj):
        cols = cols_of(g)
        return proj + lax.dot_general(
            stack[: 2 * K, cols], frames[:, cols], NT, preferred_element_type=F32
        )

    gram0 = jnp.zeros((2 * K, 4 * K), F32)
    proj0 = jnp.zeros((2 * K, T), F32)

    for it in range(ITERS):
        cg_g[it, pl.ds(gi, 1)] = jnp.zeros((1, K, BLOCK), F32)
    fold[...] = jnp.zeros((K, BLOCK), F32)
    lane = lax.broadcasted_iota(jnp.int32, (K, BLOCK), 1)
    sub = lax.broadcasted_iota(jnp.int32, (K, BLOCK), 0)
    ridge = jnp.where(lane == sub, RIDGE, 0.0)

    small[2].wait()
    small[3].wait()
    gram = lax.fori_loop(0, NG, prepare, gram0)
    pl.semaphore_wait(barrier, (NZ - 1) + (NG - 1) + (NY - 1))

    for it in range(ITERS):
        last = it == ITERS - 1

        def at(ref):
            return ref.at[it]

        fold[:, : 4 * K] = gram[:K] + gram[K:]
        gram_z[it, z] = fold[:8] + pltpu.roll(fold[8:], BLOCK // 2, 1)
        to_all(at(gram_z), at(s_gram), at(r_gram), NZ, z, z_dev)
        if it == 0:
            proj = proj0
            for g in range(NG):
                loads[g].wait()
                proj = project(g, proj)
        proj_z[it, pl.ds(z, 1)] = (proj[:K] + proj[K:])[None]
        to_all(at(proj_z), at(s_proj), at(r_proj), NZ, z, z_dev)

        if it == 0:
            tables()
        from_all(at(gram_z), at(s_gram), at(r_gram), NZ, z, z_dev)
        folded = summed(at(gram_z), NZ)
        raw = jnp.concatenate([folded, pltpu.roll(folded, BLOCK // 2, 1)], axis=0)
        dark_dot = jnp.sum(
            jnp.where((lane >= 3 * K) & (lane < 3 * K + 3), raw, 0.0), axis=1, keepdims=True
        )
        gram_f = jnp.where(lane < K, raw + pltpu.roll(raw, BLOCK - K, 1), 0.0) / pixels_all
        solver = inverse(gram_f + ridge)
        from_all(at(proj_z), at(s_proj), at(r_proj), NZ, z, z_dev)
        right = (summed(at(proj_z), NZ) - dark_dot) / pixels_all
        coef = lax.dot_general(
            solver[:, :K], right, NN, precision=HIGHEST, preferred_element_type=F32
        )
        if last:
            coef_out[...] = coef

        valid_row = valid_ref[...].astype(F32)
        c_high = coef.astype(BF16).astype(F32)
        c_stack = jnp.concatenate(
            [c_high, c_high, coef - c_high, jnp.ones((K, T), F32)], axis=0
        )
        coef_lhs[...] = (c_stack * valid_row).T.astype(BF16)

        aligned = (NX * NB) % kinds == 0

        def residual(cc, acc):
            for b in range(NX * NB):
                block = cc * (NX * NB) + b
                cols = pl.ds(pl.multiple_of(block * BLOCK, BLOCK), BLOCK)
                r = floats[:, cols] - lax.dot_general(
                    coef_lhs[...], stack[:, cols], NN, preferred_element_type=F32
                )
                kind = b % kinds if aligned else kind_of(block).astype(F32)
                if not aligned or kind < FORE_MAX:
                    r = jnp.where(limit[...] <= kind, r, 0.0)
                resid[:, cols] = r
                acc = acc + jnp.sum((r * r).reshape(T // 8, 8, BLOCK), axis=0)
            return acc

        acc = lax.fori_loop(0, NC, residual, jnp.zeros((8, BLOCK), F32))
        sq_z[it, pl.ds(z, 1)] = jnp.sum(acc, axis=0, keepdims=True)[None]
        to_all(at(sq_z), at(s_sqz), at(r_sqz), NZ, z, z_dev)

        cg = lax.dot_general(
            coef * valid_row, coef, NT, precision=HIGHEST, preferred_element_type=F32
        )
        cg_g[it, pl.ds(gi, 1), :, :K] = cg[None]
        to_all(at(cg_g), at(s_cgg), at(r_cgg), NG, gi, g_dev)
        from_all(at(cg_g), at(s_cgg), at(r_cgg), NG, gi, g_dev)
        cg_y[it, pl.ds(y, 1)] = summed(at(cg_g), NG)[None]
        to_all(at(cg_y), at(s_cgy), at(r_cgy), NY, y, y_dev)

        from_all(at(sq_z), at(s_sqz), at(r_sqz), NZ, z, z_dev)
        sq_g[it, pl.ds(gi, 1)] = summed(at(sq_z), NZ)[None]
        to_all(at(sq_g), at(s_sqg), at(r_sqg), NG, gi, g_dev)
        from_all(at(sq_g), at(s_sqg), at(r_sqg), NG, gi, g_dev)
        sq_y[it, pl.ds(y, 1)] = summed(at(sq_g), NG)[None]
        to_all(at(sq_y), at(s_sqy), at(r_sqy), NY, y, y_dev)

        from_all(at(cg_y), at(s_cgy), at(r_cgy), NY, y, y_dev)
        gram_c = jnp.where(lane < K, summed(at(cg_y), NY) / tiles_all, 0.0)
        solver_c = inverse(gram_c + ridge)
        solved = lax.dot_general(
            solver_c[:, :K], coef, NN, precision=HIGHEST, preferred_element_type=F32
        ) / tiles_all
        high, low = split2(solved)
        term_lhs[...] = jnp.concatenate([high, low], axis=0)

        from_all(at(sq_y), at(s_sqy), at(r_sqy), NY, y, y_dev)
        square = jnp.sum(summed(at(sq_y), NY), axis=1, keepdims=True)
        spread = square / (float(tiles_all) * float(pixels_all)) + 1e-05
        rate = 1.0 / (4.0 * spread)

        def terms(cc, xx):
            g = cc * NX + xx
            pair = min(2, NB)
            for first in range(0, NB, pair):
                sides = []
                for j in range(first, first + pair):
                    cols = pl.ds(pl.multiple_of(g * GW + j * BLOCK, BLOCK), BLOCK)
                    r = resid[:, cols]
                    w = 1.0 / (1.0 + r * r * rate)
                    wr = w * r
                    sides.append(wr.astype(BF16))
                    part[it, cc, xx, NY, 2 * j : 2 * j + 1, :] = jnp.sum(
                        wr, axis=0, keepdims=True
                    )
                    part[it, cc, xx, NY, 2 * j + 1 : 2 * j + 2, :] = (
                        jnp.sum(w, axis=0, keepdims=True)
                        - masked[pl.ds(kind_of(g * NB + j), 1), :]
                    )
                a = lax.dot_general(
                    term_lhs[...],
                    jnp.concatenate(sides, axis=1),
                    NN,
                    preferred_element_type=F32,
                )
                a = a[:K] + a[K:]
                for j in range(first, first + pair):
                    tile = a[:, (j - first) * BLOCK : (j - first + 1) * BLOCK]
                    part[it, cc, xx, pl.ds(2 * j, 2)] = tile.reshape(2, 8, BLOCK)

        def core_copy(xx):
            return copy(
                part.at[it, other, xx],
                from_core.at[it, xx],
                s_core.at[it],
                r_core.at[it, xx],
                c_dev(),
            )

        def x_copy(xx):
            return copy(
                x_src.at[it, xx], x_in.at[it, x], s_x.at[it], r_x.at[it], x_dev(xx)
            )

        order_x = list(reversed(near_x))
        for o in [*order_x, 0]:
            xx = lax.rem(x + o, NX)
            terms(other, xx)
            core_copy(xx).start()
        for o in [*order_x, 0]:
            xx = lax.rem(x + o, NX)
            terms(c, xx)
            core_copy(xx).wait_recv()
            both = part[it, c, xx] + from_core[it, xx]
            if o:
                x_src[it, xx] = both
                x_copy(xx).start()
            else:
                x_in[it, x] = both

        from_all(at(x_in), at(s_x), at(r_x), NX, x, x_dev)
        mine = summed(at(x_in), NX)
        y_src[it] = mine[:NY]
        sum_in[it, y] = mine[NY]
        y_in[it, y] = y_src[it, y]
        for o in reversed(near_y):
            yy = lax.rem(y + o, NY)
            copy(y_src.at[it, yy], y_in.at[it, y], at(s_y), at(r_y), y_dev(yy)).start()
        to_all(at(sum_in), at(s_t), at(r_t), NY, y, y_dev)
        from_all(at(y_in), at(s_y), at(r_y), NY, y, y_dev)
        full[it, c, x, 0] = summed(at(y_in), NY)

        def chunk_copy(xx, cut, dev, ssem, rsem):
            low, high = cuts[cut]
            where = full.at[it, c, xx, pl.ds(low, high - low)]
            return copy(where, where, ssem, rsem, dev)

        def to_core(xx, cut):
            chunk_copy(xx, cut, c_dev(), s_ca.at[it], r_ca.at[it, xx]).start()

        def onward(cut):
            for o in reversed(near_x):
                dev = x_dev(lax.rem(x + o, NX))
                chunk_copy(x, cut, dev, s_xa.at[it], r_xa.at[it, cut]).start()
            to_core(x, cut)

        for o in reversed(near_y):
            slot = slots[NY - o]
            cut = [low <= slot < high for low, high in cuts].index(True)
            copy(
                full.at[it, c, x, 0],
                full.at[it, c, x, slot],
                s_ya.at[it],
                r_ya.at[it, cut],
                y_dev(lax.rem(y + o, NY)),
            ).start()
        for cut, (low, high) in enumerate(cuts):
            if high == NY + 1:
                from_all(at(sum_in), at(s_t), at(r_t), NY, y, y_dev)
                full[it, c, x, NY] = summed(at(sum_in), NY)
            count = sum(low <= slots[o] < high for o in near_y)
            if count:
                some = full.at[it, c, x, pl.ds(0, count)]
                copy(some, some, s_ya.at[it], r_ya.at[it, cut], y_dev(lax.rem(y + 1, NY))).wait_recv()
            onward(cut)

        def apply(cc, xx):
            g = cc * NX + xx
            for j in range(NB):
                cols = pl.ds(pl.multiple_of(g * GW + j * BLOCK, BLOCK), BLOCK)
                for half in range(2):
                    rows = pl.ds(8 * half, 8)
                    delta = full[it, cc, xx, slot_of(2 * j + half)]
                    basis_out[rows, cols] = basis_out[rows, cols] + delta
                top = full[it, cc, xx, NY, 2 * j : 2 * j + 1, :]
                low = full[it, cc, xx, NY, 2 * j + 1 : 2 * j + 2, :]
                dark_out[:, cols] = dark_out[:, cols] + top / (low + 1.0)
            return g

        def take(cc, xx, carry):
            g = apply(cc, xx)
            if last:
                return carry
            gram, proj = carry
            return prepare(g, gram), project(g, proj)

        carry = 0 if last else (gram0, proj0)
        carry = take(c, x, carry)
        for cut, (low, high) in enumerate(cuts):
            some = full.at[it, c, pl.ds(0, NX - 1), pl.ds(low, high - low)]
            copy(some, some, s_xa.at[it], r_xa.at[it, cut], x_dev(lax.rem(x + 1, NX))).wait_recv()
            for o in reversed(near_x):
                to_core(lax.rem(x + o, NX), cut)

        for o in near_x:
            carry = take(c, lax.rem(x + o, NX), carry)
        for o in [0, *near_x]:
            xx = lax.rem(x + o, NX)
            where = full.at[it, other, xx]
            copy(where, where, s_ca.at[it], r_ca.at[it, xx], c_dev()).wait_recv()
            carry = take(other, xx, carry)
        if not last:
            gram, proj = carry

        for ref, sem in (
            (part.at[it, c], s_core),
            (x_src.at[it, pl.ds(0, NX - 1)], s_x),
            (y_src.at[it, pl.ds(0, NY - 1)], s_y),
            (full.at[it, c, x, pl.ds(0, NY - 1)], s_ya),
            (full.at[it, c, pl.ds(0, NX - 1)], s_xa),
            (full.at[it, c], s_ca),
        ):
            sent.append(copy(ref, ref, sem.at[it], r_core.at[it, 0], c_dev()))

    for made in sent:
        made.wait_send()


def write_kernel(*refs):
    copies = [pltpu.make_async_copy(refs[i], refs[i + 3], refs[6].at[i]) for i in range(3)]
    for made in copies:
        made.start()
    for made in copies:
        made.wait()


def local(frames, tile_valid, foreground_blocks, basis_start, dark_start):
    T, PX = frames.shape
    K = basis_start.shape[0]
    NY, NX, NC, NZ = (lax.axis_size(n) for n in (*TILES, "pix"))
    NG = NX * NC
    vmem = pl.BlockSpec(memory_space=pltpu.VMEM)
    dma = pltpu.SemaphoreType.DMA
    scratch = [
        pltpu.VMEM((T, PX), BF16),
        pltpu.VMEM((1, T), jnp.int32),
        pltpu.VMEM((1, T), jnp.int32),
        pltpu.VMEM((T, PX), F32),
        pltpu.VMEM((4 * K, PX), BF16),
        pltpu.VMEM((T, 4 * K), BF16),
        pltpu.VMEM((2 * K, T), BF16),
        pltpu.VMEM((T, BLOCK), F32),
        pltpu.VMEM((T, BLOCK), F32),
        pltpu.VMEM((T, PX), F32),
        pltpu.VMEM((ROW_PX // BLOCK, BLOCK), F32),
        pltpu.VMEM((K, BLOCK), F32),
        pltpu.VMEM((ITERS, NZ, 8, BLOCK), F32),
        pltpu.VMEM((ITERS, NZ, K, T), F32),
        pltpu.VMEM((ITERS, NZ, 1, BLOCK), F32),
        pltpu.VMEM((ITERS, NG, 1, BLOCK), F32),
        pltpu.VMEM((ITERS, NY, 1, BLOCK), F32),
        pltpu.VMEM((ITERS, NG, K, BLOCK), F32),
        pltpu.VMEM((ITERS, NY, K, BLOCK), F32),
        pltpu.VMEM((ITERS, NC, NX, NY + 1, 8, BLOCK), F32),
        pltpu.VMEM((ITERS, NX, NY + 1, 8, BLOCK), F32),
        pltpu.VMEM((ITERS, NX, NY + 1, 8, BLOCK), F32),
        pltpu.VMEM((ITERS, NX, NY + 1, 8, BLOCK), F32),
        pltpu.VMEM((ITERS, NY, 8, BLOCK), F32),
        pltpu.VMEM((ITERS, NY, 8, BLOCK), F32),
        pltpu.VMEM((ITERS, NY, 8, BLOCK), F32),
        pltpu.VMEM((ITERS, NC, NX, NY + 1, 8, BLOCK), F32),
        dma((NG,)),
        dma((4,)),
    ]
    several = len(cuts_of(NY))
    for arrivals in [()] * 7 + [(NX,)] + [()] * 3 + [(several,), (several,), (NX,)]:
        scratch += [dma((ITERS,)), dma((ITERS, *arrivals))]
    basis, dark, coef = pl.pallas_call(
        functools.partial(fit_kernel, (NY, NX, NC, NZ, T, PX, K)),
        out_shape=(
            pltpu.VMEM((K, PX), F32),
            pltpu.VMEM((1, PX), F32),
            pltpu.VMEM((K, T), F32),
        ),
        in_specs=[pl.BlockSpec(memory_space=pl.ANY)] * 5,
        out_specs=(vmem, vmem, vmem),
        scratch_shapes=scratch,
        compiler_params=pltpu.CompilerParams(
            collective_id=0, has_side_effects=True, vmem_limit_bytes=67043328 - 1400000
        ),
    )(
        frames,
        tile_valid.reshape(1, T),
        foreground_blocks.reshape(1, T),
        basis_start,
        dark_start.reshape(1, PX),
    )
    results = (basis, dark, coef)
    basis, dark, coef = pl.pallas_call(
        write_kernel,
        out_shape=tuple(jax.ShapeDtypeStruct(r.shape, r.dtype) for r in results),
        in_specs=[pl.BlockSpec(memory_space=pl.ANY)] * 3,
        out_specs=[pl.BlockSpec(memory_space=pltpu.HBM)] * 3,
        scratch_shapes=[dma((3,))],
        compiler_params=pltpu.CompilerParams(vmem_limit_bytes=1024 * 1024),
    )(*results)
    return basis, dark.reshape(PX), coef.T


def solution(mesh):
    finer = Mesh(
        mesh.devices.reshape(8, 4, 2, mesh.shape["pix"]), ("tiles_0", "tiles_1", "tiles_2", "pix")
    )
    in_specs = (P(TILES, "pix"), P(TILES), P(TILES), P(None, "pix"), P("pix"))
    out_specs = (P(None, "pix"), P("pix"), P(TILES, None))
    return jax.shard_map(local, mesh=finer, in_specs=in_specs, out_specs=out_specs, check_vma=False)
```

```python
import functools

import jax
import jax.numpy as jnp
from jax import lax
from jax.experimental import pallas as pl
from jax.experimental.pallas import tpu as pltpu
from jax.sharding import Mesh
from jax.sharding import PartitionSpec as P

ROW_PX = 2048
BLOCK = 128
ITERS = 2
FORE_MAX = 8
TILES = ("tiles_0", "tiles_1", "tiles_2")
MESH = pl.DeviceIdType.MESH
HIGHEST = lax.Precision.HIGHEST
RIDGE = 0.01
F32 = jnp.float32
BF16 = jnp.bfloat16

NT = (((1,), (1,)), ((), ()))
NN = (((1,), (0,)), ((), ()))


def split2(x):
    high = x.astype(BF16)
    low = (x - high.astype(F32)).astype(BF16)
    return high, low


def inverse(a):
    rows = a.shape[0]
    lane = lax.broadcasted_iota(jnp.int32, a.shape, 1)
    sub = lax.broadcasted_iota(jnp.int32, a.shape, 0)
    for k in range(rows):
        scale = 1.0 / a[k : k + 1, k : k + 1]
        row = jnp.where(lane[:1] == k, 1.0, a[k : k + 1, :]) * scale
        col = a[:, k : k + 1]
        a = jnp.where(sub == k, row, jnp.where(lane == k, 0.0, a) - col * row)
    return a


def cuts_of(NY):
    half = NY // 2 + 1
    return [(0, half), (half, NY + 1)]


def fit_kernel(
    sizes,
    frames_hbm,
    valid_hbm,
    fore_hbm,
    basis_hbm,
    dark_hbm,
    basis_out,
    dark_out,
    coef_out,
    frames,
    valid_ref,
    fore_ref,
    resid,
    stack,
    coef_lhs,
    term_lhs,
    limit,
    spot,
    floats,
    masked,
    fold,
    gram_z,
    proj_z,
    sq_z,
    sq_g,
    sq_y,
    cg_g,
    cg_y,
    part,
    from_core,
    x_src,
    x_in,
    y_src,
    y_in,
    sum_in,
    full,
    load_sem,
    small_sem,
    s_gram,
    r_gram,
    s_proj,
    r_proj,
    s_sqz,
    r_sqz,
    s_sqg,
    r_sqg,
    s_sqy,
    r_sqy,
    s_cgg,
    r_cgg,
    s_cgy,
    r_cgy,
    s_core,
    r_core,
    s_x,
    r_x,
    s_y,
    r_y,
    s_t,
    r_t,
    s_ya,
    r_ya,
    s_xa,
    r_xa,
    s_ca,
    r_ca,
):
    NY, NX, NC, NZ, T, PX, K = sizes
    NG = NX * NC
    GW = PX // NG
    NB = GW // BLOCK
    y, x, c, z = (lax.axis_index(n) for n in (*TILES, "pix"))
    gi = x * NC + c
    other = 1 - c
    tiles_all = T * NY * NX * NC
    pixels_all = PX * NZ

    def y_dev(yy):
        return {"tiles_0": yy}

    def x_dev(xx):
        return {"tiles_1": xx}

    def g_dev(g):
        return {"tiles_1": g // NC, "tiles_2": g % NC}

    def z_dev(zz):
        return {"pix": zz}

    def c_dev():
        return {"tiles_2": other}

    loads = [
        pltpu.make_async_copy(
            frames_hbm.at[:, pl.ds(g * GW, GW)], frames.at[:, pl.ds(g * GW, GW)], load_sem.at[g]
        )
        for g in range(NG)
    ]
    small = [
        pltpu.make_async_copy(src, dst, small_sem.at[i])
        for i, (src, dst) in enumerate(
            (
                (valid_hbm, valid_ref),
                (fore_hbm, fore_ref),
                (dark_hbm, dark_out),
                (basis_hbm, basis_out),
            )
        )
    ]
    for load in small + loads:
        load.start()

    barrier = pltpu.get_barrier_semaphore()
    for size, me, dev in ((NZ, z, z_dev), (NG, gi, g_dev), (NY, y, y_dev)):
        for o in range(1, size):
            pl.semaphore_signal(
                barrier, inc=1, device_id=dev(lax.rem(me + o, size)), device_id_type=MESH
            )

    near_y = sorted(range(1, NY), key=lambda o: min(o, NY - o))
    near_x = sorted(range(1, NX), key=lambda o: min(o, NX - o))
    slots = {0: 0, **{o: i + 1 for i, o in enumerate(near_y)}}
    cuts = cuts_of(NY)

    def slot_of(tile):
        o = lax.rem(tile - y + NY, NY)
        behind = o // (NY // 2 + 1)
        own = (NY - o) // NY
        return (1 - behind) * (2 * o - 1 + own) + behind * (2 * NY - 2 * o)

    sent = []

    def copy(src, dst, ssem, rsem, dev):
        return pltpu.make_async_remote_copy(
            src_ref=src,
            dst_ref=dst,
            send_sem=ssem,
            recv_sem=rsem,
            device_id=dev,
            device_id_type=MESH,
        )

    def whole(buf, ssem, rsem, size, me, dev):
        every = buf.at[pl.ds(0, size - 1)]
        return copy(every, every, ssem, rsem, dev(lax.rem(me + 1, size)))

    def to_all(buf, ssem, rsem, size, me, dev):
        for o in sorted(range(1, size), key=lambda o: -min(o, size - o)):
            copy(buf.at[me], buf.at[me], ssem, rsem, dev(lax.rem(me + o, size))).start()
        sent.append(whole(buf, ssem, rsem, size, me, dev))

    def from_all(buf, ssem, rsem, size, me, dev):
        whole(buf, ssem, rsem, size, me, dev).wait_recv()

    def summed(buf, size):
        total = buf[0]
        for i in range(1, size):
            total = total + buf[i]
        return total

    kinds = ROW_PX // BLOCK

    def kind_of(block):
        return lax.rem(z * (NG * NB) + block, kinds)

    def tables():
        small[0].wait()
        small[1].wait()
        valid_row = valid_ref[...].astype(F32)
        limit[...] = jnp.broadcast_to(fore_ref[...].astype(F32), (BLOCK, T)).T
        valid_tiles = jnp.broadcast_to(valid_row, (BLOCK, T)).T
        bad = 1.0 - valid_tiles
        for k in range(kinds):
            out = bad if k >= FORE_MAX else jnp.where(limit[...] > float(k), 1.0, bad)
            masked[k : k + 1, :] = jnp.sum(out, axis=0, keepdims=True)
        spot[...] = valid_tiles

        @pl.loop(0, NG * NB)
        def _(b):
            cols = pl.ds(pl.multiple_of(b * BLOCK, BLOCK), BLOCK)
            floats[:, cols] = frames[:, cols].astype(F32) * spot[...]

    row16 = lax.broadcasted_iota(jnp.int32, (16, GW), 0)

    def cols_of(g):
        return pl.ds(pl.multiple_of(g * GW, GW), GW)

    def prepare(g, gram):
        cols = cols_of(g)
        high, low = split2(basis_out[:, cols])
        d = dark_out[:, cols]
        d_high = d.astype(BF16).astype(F32)
        d_mid = (d - d_high).astype(BF16).astype(F32)
        d_low = d - d_high - d_mid
        dark_rows = jnp.where(
            row16 == 0,
            d_high,
            jnp.where(row16 == 1, d_mid, jnp.where(row16 == 2, d_low, 0.0)),
        )
        pieces = jnp.concatenate([high, low, high, dark_rows.astype(BF16)], axis=0)
        stack[:, cols] = pieces
        return gram + lax.dot_general(pieces[: 2 * K], pieces, NT, preferred_element_type=F32)

    def project(g, proj):
        cols = cols_of(g)
        return proj + lax.dot_general(
            stack[: 2 * K, cols], frames[:, cols], NT, preferred_element_type=F32
        )

    gram0 = jnp.zeros((2 * K, 4 * K), F32)
    proj0 = jnp.zeros((2 * K, T), F32)

    for it in range(ITERS):
        cg_g[it, pl.ds(gi, 1)] = jnp.zeros((1, K, BLOCK), F32)
    fold[...] = jnp.zeros((K, BLOCK), F32)
    lane = lax.broadcasted_iota(jnp.int32, (K, BLOCK), 1)
    sub = lax.broadcasted_iota(jnp.int32, (K, BLOCK), 0)
    ridge = jnp.where(lane == sub, RIDGE, 0.0)

    small[2].wait()
    small[3].wait()
    gram = lax.fori_loop(0, NG, prepare, gram0)
    pl.semaphore_wait(barrier, (NZ - 1) + (NG - 1) + (NY - 1))

    for it in range(ITERS):
        last = it == ITERS - 1

        def at(ref):
            return ref.at[it]

        fold[:, : 4 * K] = gram[:K] + gram[K:]
        gram_z[it, z] = fold[:8] + pltpu.roll(fold[8:], BLOCK // 2, 1)
        to_all(at(gram_z), at(s_gram), at(r_gram), NZ, z, z_dev)
        if it == 0:
            proj = proj0
            for g in range(NG):
                loads[g].wait()
                proj = project(g, proj)
        proj_z[it, pl.ds(z, 1)] = (proj[:K] + proj[K:])[None]
        to_all(at(proj_z), at(s_proj), at(r_proj), NZ, z, z_dev)

        if it == 0:
            tables()
        from_all(at(gram_z), at(s_gram), at(r_gram), NZ, z, z_dev)
        folded = summed(at(gram_z), NZ)
        raw = jnp.concatenate([folded, pltpu.roll(folded, BLOCK // 2, 1)], axis=0)
        dark_dot = jnp.sum(
            jnp.where((lane >= 3 * K) & (lane < 3 * K + 3), raw, 0.0), axis=1, keepdims=True
        )
        gram_f = jnp.where(lane < K, raw + pltpu.roll(raw, BLOCK - K, 1), 0.0) / pixels_all
        solver = inverse(gram_f + ridge)
        from_all(at(proj_z), at(s_proj), at(r_proj), NZ, z, z_dev)
        right = (summed(at(proj_z), NZ) - dark_dot) / pixels_all
        coef = lax.dot_general(
            solver[:, :K], right, NN, precision=HIGHEST, preferred_element_type=F32
        )
        if last:
            coef_out[...] = coef

        valid_row = valid_ref[...].astype(F32)
        c_high = coef.astype(BF16).astype(F32)
        c_stack = jnp.concatenate(
            [c_high, c_high, coef - c_high, jnp.ones((K, T), F32)], axis=0
        )
        coef_lhs[...] = (c_stack * valid_row).T.astype(BF16)

        aligned = (NX * NB) % kinds == 0

        def residual(cc, acc):
            for b in range(NX * NB):
                block = cc * (NX * NB) + b
                cols = pl.ds(pl.multiple_of(block * BLOCK, BLOCK), BLOCK)
                r = floats[:, cols] - lax.dot_general(
                    coef_lhs[...], stack[:, cols], NN, preferred_element_type=F32
                )
                kind = b % kinds if aligned else kind_of(block).astype(F32)
                if not aligned or kind < FORE_MAX:
                    r = jnp.where(limit[...] <= kind, r, 0.0)
                resid[:, cols] = r
                acc = acc + jnp.sum((r * r).reshape(T // 8, 8, BLOCK), axis=0)
            return acc

        acc = lax.fori_loop(0, NC, residual, jnp.zeros((8, BLOCK), F32))
        sq_z[it, pl.ds(z, 1)] = jnp.sum(acc, axis=0, keepdims=True)[None]
        to_all(at(sq_z), at(s_sqz), at(r_sqz), NZ, z, z_dev)

        cg = lax.dot_general(
            coef * valid_row, coef, NT, precision=HIGHEST, preferred_element_type=F32
        )
        cg_g[it, pl.ds(gi, 1), :, :K] = cg[None]
        to_all(at(cg_g), at(s_cgg), at(r_cgg), NG, gi, g_dev)
        from_all(at(cg_g), at(s_cgg), at(r_cgg), NG, gi, g_dev)
        cg_y[it, pl.ds(y, 1)] = summed(at(cg_g), NG)[None]
        to_all(at(cg_y), at(s_cgy), at(r_cgy), NY, y, y_dev)

        from_all(at(sq_z), at(s_sqz), at(r_sqz), NZ, z, z_dev)
        sq_g[it, pl.ds(gi, 1)] = summed(at(sq_z), NZ)[None]
        to_all(at(sq_g), at(s_sqg), at(r_sqg), NG, gi, g_dev)
        from_all(at(sq_g), at(s_sqg), at(r_sqg), NG, gi, g_dev)
        sq_y[it, pl.ds(y, 1)] = summed(at(sq_g), NG)[None]
        to_all(at(sq_y), at(s_sqy), at(r_sqy), NY, y, y_dev)

        from_all(at(cg_y), at(s_cgy), at(r_cgy), NY, y, y_dev)
        gram_c = jnp.where(lane < K, summed(at(cg_y), NY) / tiles_all, 0.0)
        solver_c = inverse(gram_c + ridge)
        solved = lax.dot_general(
            solver_c[:, :K], coef, NN, precision=HIGHEST, preferred_element_type=F32
        ) / tiles_all
        high, low = split2(solved)
        term_lhs[...] = jnp.concatenate([high, low], axis=0)

        from_all(at(sq_y), at(s_sqy), at(r_sqy), NY, y, y_dev)
        square = jnp.sum(summed(at(sq_y), NY), axis=1, keepdims=True)
        spread = square / (float(tiles_all) * float(pixels_all)) + 1e-05
        knee = 4.0 * spread

        def terms(cc, xx):
            g = cc * NX + xx
            pair = min(2, NB)
            for first in range(0, NB, pair):
                sides = []
                for j in range(first, first + pair):
                    cols = pl.ds(pl.multiple_of(g * GW + j * BLOCK, BLOCK), BLOCK)
                    r = resid[:, cols]
                    w = 1.0 / (knee + r * r)
                    wr = w * r
                    sides.append(wr.astype(BF16))
                    part[it, cc, xx, NY, 2 * j : 2 * j + 1, :] = knee * jnp.sum(
                        wr, axis=0, keepdims=True
                    )
                    part[it, cc, xx, NY, 2 * j + 1 : 2 * j + 2, :] = (
                        knee * jnp.sum(w, axis=0, keepdims=True)
                        - masked[pl.ds(kind_of(g * NB + j), 1), :]
                    )
                a = lax.dot_general(
                    term_lhs[...],
                    jnp.concatenate(sides, axis=1),
                    NN,
                    preferred_element_type=F32,
                )
                a = knee * (a[:K] + a[K:])
                for j in range(first, first + pair):
                    tile = a[:, (j - first) * BLOCK : (j - first + 1) * BLOCK]
                    part[it, cc, xx, pl.ds(2 * j, 2)] = tile.reshape(2, 8, BLOCK)

        def core_copy(xx):
            return copy(
                part.at[it, other, xx],
                from_core.at[it, xx],
                s_core.at[it],
                r_core.at[it, xx],
                c_dev(),
            )

        def x_copy(xx):
            return copy(
                x_src.at[it, xx], x_in.at[it, x], s_x.at[it], r_x.at[it], x_dev(xx)
            )

        order_x = list(reversed(near_x))
        for o in [*order_x, 0]:
            xx = lax.rem(x + o, NX)
            terms(other, xx)
            core_copy(xx).start()
        for o in [*order_x, 0]:
            xx = lax.rem(x + o, NX)
            terms(c, xx)
            core_copy(xx).wait_recv()
            both = part[it, c, xx] + from_core[it, xx]
            if o:
                x_src[it, xx] = both
                x_copy(xx).start()
            else:
                x_in[it, x] = both

        from_all(at(x_in), at(s_x), at(r_x), NX, x, x_dev)
        mine = summed(at(x_in), NX)
        y_src[it] = mine[:NY]
        sum_in[it, y] = mine[NY]
        y_in[it, y] = y_src[it, y]
        for o in reversed(near_y):
            yy = lax.rem(y + o, NY)
            copy(y_src.at[it, yy], y_in.at[it, y], at(s_y), at(r_y), y_dev(yy)).start()
        to_all(at(sum_in), at(s_t), at(r_t), NY, y, y_dev)
        from_all(at(y_in), at(s_y), at(r_y), NY, y, y_dev)
        full[it, c, x, 0] = summed(at(y_in), NY)

        def chunk_copy(xx, cut, dev, ssem, rsem):
            low, high = cuts[cut]
            where = full.at[it, c, xx, pl.ds(low, high - low)]
            return copy(where, where, ssem, rsem, dev)

        def to_core(xx, cut):
            chunk_copy(xx, cut, c_dev(), s_ca.at[it], r_ca.at[it, xx]).start()

        def onward(cut):
            for o in reversed(near_x):
                dev = x_dev(lax.rem(x + o, NX))
                chunk_copy(x, cut, dev, s_xa.at[it], r_xa.at[it, cut]).start()
            to_core(x, cut)

        for o in reversed(near_y):
            slot = slots[NY - o]
            cut = [low <= slot < high for low, high in cuts].index(True)
            copy(
                full.at[it, c, x, 0],
                full.at[it, c, x, slot],
                s_ya.at[it],
                r_ya.at[it, cut],
                y_dev(lax.rem(y + o, NY)),
            ).start()
        for cut, (low, high) in enumerate(cuts):
            if high == NY + 1:
                from_all(at(sum_in), at(s_t), at(r_t), NY, y, y_dev)
                full[it, c, x, NY] = summed(at(sum_in), NY)
            count = sum(low <= slots[o] < high for o in near_y)
            if count:
                some = full.at[it, c, x, pl.ds(0, count)]
                copy(some, some, s_ya.at[it], r_ya.at[it, cut], y_dev(lax.rem(y + 1, NY))).wait_recv()
            onward(cut)

        def apply(cc, xx):
            g = cc * NX + xx
            for j in range(NB):
                cols = pl.ds(pl.multiple_of(g * GW + j * BLOCK, BLOCK), BLOCK)
                for half in range(2):
                    rows = pl.ds(8 * half, 8)
                    delta = full[it, cc, xx, slot_of(2 * j + half)]
                    basis_out[rows, cols] = basis_out[rows, cols] + delta
                top = full[it, cc, xx, NY, 2 * j : 2 * j + 1, :]
                low = full[it, cc, xx, NY, 2 * j + 1 : 2 * j + 2, :]
                dark_out[:, cols] = dark_out[:, cols] + top / (low + 1.0)
            return g

        def take(cc, xx, carry):
            g = apply(cc, xx)
            if last:
                return carry
            gram, proj = carry
            return prepare(g, gram), project(g, proj)

        carry = 0 if last else (gram0, proj0)
        carry = take(c, x, carry)
        for cut, (low, high) in enumerate(cuts):
            some = full.at[it, c, pl.ds(0, NX - 1), pl.ds(low, high - low)]
            copy(some, some, s_xa.at[it], r_xa.at[it, cut], x_dev(lax.rem(x + 1, NX))).wait_recv()
            for o in reversed(near_x):
                to_core(lax.rem(x + o, NX), cut)

        for o in near_x:
            carry = take(c, lax.rem(x + o, NX), carry)
        for o in [0, *near_x]:
            xx = lax.rem(x + o, NX)
            where = full.at[it, other, xx]
            copy(where, where, s_ca.at[it], r_ca.at[it, xx], c_dev()).wait_recv()
            carry = take(other, xx, carry)
        if not last:
            gram, proj = carry

        for ref, sem in (
            (part.at[it, c], s_core),
            (x_src.at[it, pl.ds(0, NX - 1)], s_x),
            (y_src.at[it, pl.ds(0, NY - 1)], s_y),
            (full.at[it, c, x, pl.ds(0, NY - 1)], s_ya),
            (full.at[it, c, pl.ds(0, NX - 1)], s_xa),
            (full.at[it, c], s_ca),
        ):
            sent.append(copy(ref, ref, sem.at[it], r_core.at[it, 0], c_dev()))

    for made in sent:
        made.wait_send()


def write_kernel(*refs):
    copies = [pltpu.make_async_copy(refs[i], refs[i + 3], refs[6].at[i]) for i in range(3)]
    for made in copies:
        made.start()
    for made in copies:
        made.wait()


def local(frames, tile_valid, foreground_blocks, basis_start, dark_start):
    T, PX = frames.shape
    K = basis_start.shape[0]
    NY, NX, NC, NZ = (lax.axis_size(n) for n in (*TILES, "pix"))
    NG = NX * NC
    vmem = pl.BlockSpec(memory_space=pltpu.VMEM)
    dma = pltpu.SemaphoreType.DMA
    scratch = [
        pltpu.VMEM((T, PX), BF16),
        pltpu.VMEM((1, T), jnp.int32),
        pltpu.VMEM((1, T), jnp.int32),
        pltpu.VMEM((T, PX), F32),
        pltpu.VMEM((4 * K, PX), BF16),
        pltpu.VMEM((T, 4 * K), BF16),
        pltpu.VMEM((2 * K, T), BF16),
        pltpu.VMEM((T, BLOCK), F32),
        pltpu.VMEM((T, BLOCK), F32),
        pltpu.VMEM((T, PX), F32),
        pltpu.VMEM((ROW_PX // BLOCK, BLOCK), F32),
        pltpu.VMEM((K, BLOCK), F32),
        pltpu.VMEM((ITERS, NZ, 8, BLOCK), F32),
        pltpu.VMEM((ITERS, NZ, K, T), F32),
        pltpu.VMEM((ITERS, NZ, 1, BLOCK), F32),
        pltpu.VMEM((ITERS, NG, 1, BLOCK), F32),
        pltpu.VMEM((ITERS, NY, 1, BLOCK), F32),
        pltpu.VMEM((ITERS, NG, K, BLOCK), F32),
        pltpu.VMEM((ITERS, NY, K, BLOCK), F32),
        pltpu.VMEM((ITERS, NC, NX, NY + 1, 8, BLOCK), F32),
        pltpu.VMEM((ITERS, NX, NY + 1, 8, BLOCK), F32),
        pltpu.VMEM((ITERS, NX, NY + 1, 8, BLOCK), F32),
        pltpu.VMEM((ITERS, NX, NY + 1, 8, BLOCK), F32),
        pltpu.VMEM((ITERS, NY, 8, BLOCK), F32),
        pltpu.VMEM((ITERS, NY, 8, BLOCK), F32),
        pltpu.VMEM((ITERS, NY, 8, BLOCK), F32),
        pltpu.VMEM((ITERS, NC, NX, NY + 1, 8, BLOCK), F32),
        dma((NG,)),
        dma((4,)),
    ]
    several = len(cuts_of(NY))
    for arrivals in [()] * 7 + [(NX,)] + [()] * 3 + [(several,), (several,), (NX,)]:
        scratch += [dma((ITERS,)), dma((ITERS, *arrivals))]
    basis, dark, coef = pl.pallas_call(
        functools.partial(fit_kernel, (NY, NX, NC, NZ, T, PX, K)),
        out_shape=(
            pltpu.VMEM((K, PX), F32),
            pltpu.VMEM((1, PX), F32),
            pltpu.VMEM((K, T), F32),
        ),
        in_specs=[pl.BlockSpec(memory_space=pl.ANY)] * 5,
        out_specs=(vmem, vmem, vmem),
        scratch_shapes=scratch,
        compiler_params=pltpu.CompilerParams(
            collective_id=0, has_side_effects=True, vmem_limit_bytes=67043328 - 1400000
        ),
    )(
        frames,
        tile_valid.reshape(1, T),
        foreground_blocks.reshape(1, T),
        basis_start,
        dark_start.reshape(1, PX),
    )
    results = (basis, dark, coef)
    basis, dark, coef = pl.pallas_call(
        write_kernel,
        out_shape=tuple(jax.ShapeDtypeStruct(r.shape, r.dtype) for r in results),
        in_specs=[pl.BlockSpec(memory_space=pl.ANY)] * 3,
        out_specs=[pl.BlockSpec(memory_space=pltpu.HBM)] * 3,
        scratch_shapes=[dma((3,))],
        compiler_params=pltpu.CompilerParams(vmem_limit_bytes=1024 * 1024),
    )(*results)
    return basis, dark.reshape(PX), coef.T


def solution(mesh):
    finer = Mesh(
        mesh.devices.reshape(8, 4, 2, mesh.shape["pix"]), ("tiles_0", "tiles_1", "tiles_2", "pix")
    )
    in_specs = (P(TILES, "pix"), P(TILES), P(TILES), P(None, "pix"), P("pix"))
    out_specs = (P(None, "pix"), P("pix"), P(TILES, None))
    return jax.shard_map(local, mesh=finer, in_specs=in_specs, out_specs=out_specs, check_vma=False)
```
